32 devices in a mesh: heads: 4 (over y, x), seq: 8 (over z, core).
Axes of the slice: x: 2, y: 2, z: 4, core: 2. Of those that a mesh axis runs over, the one named last changes fastest.
Arguments:
- query_rows: bfloat16 [4096, 8, 128], P('seq', 'heads'), may hold values from -16 to 16
- key_rows: bfloat16 [4096, 8, 128], P('seq', 'heads'), may hold values from -5 to 5
- value_rows: bfloat16 [4096, 8, 128], P('seq', 'heads'), may hold values from -40 to 40
- level_pick: int32 [4096], P('seq'), may hold values from 0 to 7
- level_table: float32 [8, 8, 13], P(None, 'heads'), may hold values from 0 to 3, as said below
- norm_gain: float32 [8, 128], P('heads'), may hold values from 0.5 to 1.5
- out_grad: bfloat16 [4096, 8, 128], P('seq', 'heads'), may hold values from -6 to 6
Outputs:
- normed: float32 [4096, 8, 128], P('seq', 'heads')
- query_grad: float32 [4096, 8, 128], P('seq', 'heads')
- key_grad: float32 [4096, 8, 128], P('seq', 'heads')
- value_grad: float32 [4096, 8, 128], P('seq', 'heads')
The draws below stay inside these ranges and needn't reach their ends.
Inputs may be any that keep to these rules, and one draw needn't show every extreme that they name: `level_table`: positive weights.
All inputs are finite; a program needn't handle non-finite values.
Results may differ from the reference program's by a relative error of at most 0.007.
Values sent between devices are 32-bit elements; how exact they have to be, the bound alone decides.
No kernel may reach another device: no remote copies, remote signals or barrier semaphores. Data moves between devices by JAX's collectives and lax.ppermute only.
A program may use at most 64 MiB of HBM per device.

```python
import math
import jax
import jax.numpy as jnp
from jax import lax

HEAD_DIM = 128
HEAD_DEV = 2
TOK_DEV = 512
GROUPS = 8
HEADS = 8
TOKENS = 4096
LOCAL_BITS = 9
SEQ_BITS = 3
LEVELS = 13
N_SEQ = 8


def draw_query_rows(key, part):
    noise_key = jax.random.fold_in(key, 11)
    scale_key = jax.random.fold_in(key, 12)
    values = jnp.clip(jax.random.normal(noise_key, (TOKENS, HEADS, HEAD_DIM), jnp.float32), -4.0, 4.0)
    spread = jax.random.uniform(scale_key, (TOKENS, 1, 1), jnp.float32, math.log(0.4), math.log(4.0))
    return (values * jnp.exp(spread)).astype(jnp.bfloat16)


def draw_value_rows(key, part):
    noise_key = jax.random.fold_in(key, 21)
    column_key = jax.random.fold_in(key, 22)
    head_groups = HEADS // HEAD_DEV
    head_index = (jnp.arange(HEADS, dtype=jnp.int32) // HEAD_DEV).astype(jnp.float32)
    ratio = head_index / max(head_groups - 1, 1)
    values = jnp.clip(jax.random.normal(noise_key, (TOKENS, HEADS, HEAD_DIM), jnp.float32), -4.0, 4.0)
    rising = jnp.power(3.0, 0.5 * ratio)
    columns = jnp.exp(jax.random.uniform(column_key, (HEADS, HEAD_DIM), jnp.float32, math.log(0.3), math.log(3.0)))
    return (values * columns[None] * rising[None, :, None]).astype(jnp.bfloat16)


def draw_level_table(key, part):
    level_index = jnp.arange(LEVELS, dtype=jnp.int32).astype(jnp.float32)
    shrink = jnp.power(2.0, -0.5 * jnp.maximum(level_index - 1.0, 0.0))
    factor = jnp.exp(jax.random.uniform(key, (GROUPS, HEADS, LEVELS), jnp.float32, math.log(0.5), math.log(2.0)))
    return factor * shrink[None, None, :]


def with_ends(values, rng, least, largest):
    longest = values.shape.index(max(values.shape))
    spots = []
    for shift in (0, 1):
        where = [jax.random.randint(jax.random.fold_in(rng, axis), (), 0, length) for axis, length in enumerate(values.shape)]
        where[longest] = (where[longest] + shift) % values.shape[longest]
        spots.append(tuple(where))
    return values.at[spots[0]].set(least).at[spots[1]].set(largest)


def shard_levels(rng, dims, shards, smallest, top_value):
    level, own = 1.0, jax.random.fold_in(rng, 6)
    for position, blocks in shards:
        steps = jnp.exp(jax.random.uniform(jax.random.fold_in(own, position), (blocks,), jnp.float32, smallest / len(shards), top_value / len(shards)))
        level = level * jnp.repeat(steps, dims[position] // blocks).reshape([-1 if axis == position else 1 for axis in range(len(dims))])
    return level


def noise(key, shape, scale, limit, cuts=(), kind=jnp.bfloat16):
    gain = shard_levels(key, shape, cuts, -0.22, 0.18) if cuts else 1.0
    values = jax.random.normal(key, shape, jnp.float32) * scale * gain
    return jnp.minimum(jnp.maximum(values, -limit), limit).astype(kind)


def setup_inputs(seed: int = 0) -> dict:
    keys = jax.random.split(jax.random.key(seed), 8)
    query_rows = draw_query_rows(jax.random.fold_in(keys[7], 71), 0)
    key_rows = noise(keys[1], (TOKENS, HEADS, HEAD_DIM), 1.0, 5.0, ((0, 8), (1, 4)))
    value_rows = draw_value_rows(jax.random.fold_in(keys[7], 71), 0)
    level_pick = with_ends(jax.random.randint(keys[3], (TOKENS,), 0, GROUPS), jax.random.fold_in(keys[3], 1), 0, GROUPS - 1).astype(jnp.int32)
    level_table = draw_level_table(jax.random.fold_in(keys[7], 71), 0)
    norm_gain = jnp.clip(1.0 + 0.1 * jax.random.normal(keys[5], (HEADS, HEAD_DIM), jnp.float32), 0.5, 1.5)
    out_grad = noise(keys[6], (TOKENS, HEADS, HEAD_DIM), 1.0, 6.0, ((0, 8), (1, 4)))
    return {"query_rows": query_rows, "key_rows": key_rows, "value_rows": value_rows, "level_pick": level_pick, "level_table": level_table, "norm_gain": norm_gain, "out_grad": out_grad}


exact_mode = lax.Precision.HIGHEST
epsilon = 1e-06

def bit_length(value, bits):
    value = value.astype(jnp.int32)
    result = jnp.zeros(value.shape, jnp.int32)
    for place in range(bits):
        result = result + (value >> place > 0).astype(jnp.int32)
    return result

def level_weights(token_weights, row_position, column_position, local_bits):
    level = bit_length(row_position[:, None] ^ column_position[None, :], local_bits)
    causal = column_position[None, :] <= row_position[:, None]
    weight = jnp.zeros((token_weights.shape[1], row_position.shape[0], column_position.shape[0]), jnp.float32)
    for level_no in range(local_bits + 1):
        chosen = jnp.logical_and(level == level_no, causal)
        weight = weight + jnp.where(chosen[None], jnp.transpose(token_weights[:, :, level_no])[:, :, None], 0.0)
    return weight

def sibling_select(owner, others, bits):
    layers = []
    for place in range(bits):
        owner_high = owner >> place
        layers.append(jnp.logical_and(owner_high & 1 == 1, others >> place == owner_high ^ 1).astype(jnp.float32))
    return jnp.stack(layers)

def local_forward(query_block, key_block, value_block, token_weights, local_bits, scale):
    length = query_block.shape[0]
    tile = min(512, length)
    pieces = []
    for row_block in range(length // tile):
        start = row_block * tile
        finish = start + tile
        weight = level_weights(token_weights[start:finish], jnp.arange(start, finish, dtype=jnp.int32), jnp.arange(finish, dtype=jnp.int32), local_bits)
        scores = jnp.einsum('thd,shd->hts', query_block[start:finish].astype(jnp.float32), key_block[:finish].astype(jnp.float32))
        probs = (scores * scale * weight).astype(jnp.bfloat16)
        pieces.append(jnp.einsum('hts,shd->thd', probs.astype(jnp.float32), value_block[:finish].astype(jnp.float32)))
    return jnp.concatenate(pieces, axis=0)

def local_backward(query_block, key_block, value_block, grad_block, token_weights, local_bits, scale):
    length, heads, width = query_block.shape
    tile = min(512, length)
    query_pieces = []
    key_part = jnp.zeros((length, heads, width), jnp.float32)
    value_part = jnp.zeros((length, heads, width), jnp.float32)
    for row_block in range(length // tile):
        start = row_block * tile
        finish = start + tile
        query_tile = query_block[start:finish].astype(jnp.float32)
        grad_tile = grad_block[start:finish].astype(jnp.float32)
        key_cols = key_block[:finish].astype(jnp.float32)
        value_cols = value_block[:finish].astype(jnp.float32)
        weight = level_weights(token_weights[start:finish], jnp.arange(start, finish, dtype=jnp.int32), jnp.arange(finish, dtype=jnp.int32), local_bits)
        scores = jnp.einsum('thd,shd->hts', query_tile, key_cols)
        probs = (scores * scale * weight).astype(jnp.bfloat16)
        dprob = jnp.einsum('the,she->hts', grad_tile, value_cols)
        weighted = (dprob * scale * weight).astype(jnp.bfloat16)
        query_pieces.append(jnp.einsum('hts,shd->thd', weighted.astype(jnp.float32), key_cols))
        key_part = key_part.at[:finish].add(jnp.einsum('hts,thd->shd', weighted.astype(jnp.float32), query_tile))
        value_part = value_part.at[:finish].add(jnp.einsum('hts,the->she', probs.astype(jnp.float32), grad_tile))
    return (jnp.concatenate(query_pieces, axis=0), key_part, value_part)

def reference(query_rows, key_rows, value_rows, level_pick, level_table, norm_gain, out_grad):
    scale = HEAD_DIM ** (-0.5)
    blocks = N_SEQ
    block_shape = (blocks, TOK_DEV, HEADS, HEAD_DIM)
    token_weights = level_table[level_pick]
    query_blocks = query_rows.reshape(block_shape)
    key_blocks = key_rows.reshape(block_shape)
    value_blocks = value_rows.reshape(block_shape)
    weight_blocks = token_weights.reshape(blocks, TOK_DEV, HEADS, LEVELS)
    block_ids = jnp.arange(blocks, dtype=jnp.int32)
    select = sibling_select(block_ids[:, None], block_ids[None, :], SEQ_BITS)
    own_states = jnp.einsum('bshd,bshe->bhde', key_blocks.astype(jnp.float32), value_blocks.astype(jnp.float32))
    states = jnp.einsum('jbn,nhde->bjhde', select, own_states, precision=exact_mode)
    held = states.astype(jnp.bfloat16)

    def forward_block(inputs):
        query_block, key_block, value_block, weight_block, held_block = inputs
        inner = local_forward(query_block, key_block, value_block, weight_block, LOCAL_BITS, scale)
        cross = jnp.einsum('thd,jhde->jthe', query_block.astype(jnp.float32), held_block.astype(jnp.float32))
        upper = jnp.moveaxis(weight_block[:, :, LOCAL_BITS + 1:], 2, 0)
        return inner + scale * lax.optimization_barrier(jnp.sum(upper[..., None] * cross, axis=0))
    attn = lax.map(forward_block, (query_blocks, key_blocks, value_blocks, weight_blocks, held)).reshape(TOKENS, HEADS, HEAD_DIM)
    features = HEADS * HEAD_DIM
    inverse_rms = lax.rsqrt(lax.optimization_barrier(jnp.sum(attn * attn, axis=(1, 2))) / features + epsilon)
    normed = attn * inverse_rms[:, None, None] * norm_gain[None]
    gain_grad = out_grad.astype(jnp.float32) * norm_gain[None]
    projection = lax.optimization_barrier(jnp.sum(gain_grad * attn, axis=(1, 2))) / features
    attn_grad = (inverse_rms[:, None, None] * gain_grad - attn * (inverse_rms ** 3)[:, None, None] * projection[:, None, None]).astype(jnp.bfloat16)
    grad_blocks = attn_grad.reshape(block_shape)

    def backward_block(inputs):
        query_block, key_block, value_block, weight_block, held_block, grad_block, block_id = inputs
        query_part, key_part, value_part = local_backward(query_block, key_block, value_block, grad_block, weight_block, LOCAL_BITS, scale)
        upper = jnp.moveaxis(weight_block[:, :, LOCAL_BITS + 1:], 2, 0)
        cross_back = jnp.einsum('the,jhde->jthd', grad_block.astype(jnp.float32), held_block.astype(jnp.float32))
        query_part = query_part + scale * lax.optimization_barrier(jnp.sum(upper[..., None] * cross_back, axis=0))
        scaled = (scale * upper[..., None] * grad_block.astype(jnp.float32)[None]).astype(jnp.bfloat16)
        flags = (block_id >> jnp.arange(SEQ_BITS, dtype=jnp.int32) & 1).astype(jnp.float32)
        state_grad = jnp.einsum('thd,jthe->jhde', query_block.astype(jnp.float32), scaled.astype(jnp.float32)) * flags[:, None, None, None]
        return (query_part, key_part, value_part, state_grad)
    query_part, key_part, value_part, state_grads = lax.map(backward_block, (query_blocks, key_blocks, value_blocks, weight_blocks, held, grad_blocks, block_ids))
    back = jnp.einsum('jbn,bjhde->nhde', select, state_grads, precision=exact_mode)
    back_held = back.astype(jnp.bfloat16).astype(jnp.float32)
    key_grad = key_part + jnp.einsum('bshe,bhde->bshd', value_blocks.astype(jnp.float32), back_held)
    value_grad = value_part + jnp.einsum('bshd,bhde->bshe', key_blocks.astype(jnp.float32), back_held)
    return (normed, query_part.reshape(TOKENS, HEADS, HEAD_DIM), key_grad.reshape(TOKENS, HEADS, HEAD_DIM), value_grad.reshape(TOKENS, HEADS, HEAD_DIM))
```

```python
import functools

import jax
import jax.numpy as jnp
from jax import lax
from jax.experimental import pallas as pl
from jax.experimental.pallas import tpu as pltpu
from jax.sharding import PartitionSpec as P

exact_mode = lax.Precision.HIGHEST
epsilon = 1e-06
F32 = jnp.float32
BF16 = jnp.bfloat16
VMEM = pl.BlockSpec(memory_space=pltpu.VMEM)
SMEM = pl.BlockSpec(memory_space=pltpu.SMEM)
NT = (((1,), (1,)), ((), ()))
TN = (((0,), (0,)), ((), ()))
NN = (((1,), (0,)), ((), ()))


def dot(left, right, dims):
    return lax.dot_general(left, right, dims, preferred_element_type=F32)


def swapped(block, axis, distance):
    count = lax.axis_size(axis)
    route = []
    for low in range(count):
        high = low | 1 << distance
        if high != low and high < count:
            route += [(low, high), (high, low)]
    return lax.ppermute(block, axis, route)


def summands(block, axis):
    count = lax.axis_size(axis)
    result = [block]
    for step in range(1, count):
        if count & (count - 1) == 0:
            route = [(i, i ^ step) for i in range(count)]
        else:
            route = [(i, (i + step) % count) for i in range(count)]
        result.append(lax.ppermute(block, axis, route))
    return result


def call(kernel, out_shape, args, specs, scratch=(), flops=0, name=None):
    return pl.pallas_call(
        kernel,
        out_shape=out_shape,
        in_specs=specs,
        out_specs=jax.tree.map(lambda _: VMEM, out_shape),
        scratch_shapes=list(scratch),
        compiler_params=pltpu.CompilerParams(vmem_limit_bytes=24 << 20),
        cost_estimate=pl.CostEstimate(
            flops=flops,
            transcendentals=0,
            bytes_accessed=sum(a.size * a.dtype.itemsize for a in args),
        ),
        name=name,
    )(*args)


def split_heads(source, wide, heads, length, store):
    wide[...] = source[...].astype(F32)
    for head in range(heads):
        store(head, wide[pl.ds(head, length, stride=heads), :])


def local_forward(sizes, q_ref, k_ref, v_ref, g_ref, tw_ref, gain_ref,
                  inner_ref, p_ref, w_ref, qd_ref, kd_ref, vd_ref, gg_ref, wide):
    heads, length, levels, block = sizes
    base = block.bit_length() - 1
    for source, target in ((q_ref, qd_ref), (k_ref, kd_ref), (v_ref, vd_ref)):
        def store(head, value, target=target):
            target[head] = value.astype(BF16)
        split_heads(source, wide, heads, length, store)

    def store_gain(head, value):
        gg_ref[head] = value * gain_ref[head:head + 1, :]
    split_heads(g_ref, wide, heads, length, store_gain)
    row = lax.broadcasted_iota(jnp.int32, (block, block), 0)
    column = lax.broadcasted_iota(jnp.int32, (block, block), 1)
    differs = row ^ column
    below = column <= row
    for head in range(heads):
        for i in range(length // block):
            rows = slice(i * block, (i + 1) * block)
            reach = slice(0, (i + 1) * block)
            def weight(level):
                at = head * levels + level
                return tw_ref[rows, at:at + 1]
            diagonal = jnp.broadcast_to(weight(0), (block, block))
            for level in range(1, base + 1):
                diagonal = jnp.where(differs >= 1 << (level - 1), weight(level), diagonal)
            diagonal = jnp.where(below, diagonal, 0.0)
            w_ref[head * (length // block) + i] = diagonal
            scores = dot(qd_ref[head, rows, :], kd_ref[head, reach, :], NT)
            parts = []
            for j in range(i):
                parts.append(scores[:, j * block:(j + 1) * block] * weight(base + (i ^ j).bit_length()))
            parts.append(scores[:, rows] * diagonal)
            for j, part in enumerate(parts):
                p_ref[head, rows, j * block:(j + 1) * block] = part.astype(BF16)
            inner_ref[head, rows, :] = dot(p_ref[head, rows, reach], vd_ref[head, reach, :], NN)


def join(core_ref, mine_ref, other_ref, target_ref, first, lead=None):
    half = mine_ref.shape[-3]
    core = core_ref[0]
    for h in range(half):
        for source, start in ((mine_ref, core * half), (other_ref, (1 - core) * half)):
            if lead is None:
                target_ref[start + h] = source[h].astype(target_ref.dtype)
            else:
                target_ref[first, start + h] = source[h].astype(target_ref.dtype)


def cross_kernel(sizes, *refs):
    heads, length, levels, block, bits = sizes
    core_ref, inner_ref, qd_ref, gg_ref, tw_ref, near_ref = refs[:6]
    halves = refs[6:6 + 2 * (bits - 1)]
    attn_ref, sums_ref, held_ref = refs[6 + 2 * (bits - 1):]
    held_ref[0] = near_ref[...].astype(BF16)
    for j in range(1, bits):
        join(core_ref, halves[2 * j - 2], halves[2 * j - 1], held_ref, j, lead=True)
    for i in range(length // block):
        rows = slice(i * block, (i + 1) * block)
        squares = 0.0
        products = 0.0
        for head in range(heads):
            total = inner_ref[head, rows, :]
            query = qd_ref[head, rows, :]
            for j in range(bits):
                at = head * levels + levels - bits + j
                total = total + tw_ref[rows, at:at + 1] * dot(query, held_ref[j, head], NN)
            attn_ref[head, rows, :] = total
            squares = squares + total * total
            products = products + total * gg_ref[head, rows, :]
        sums_ref[0:1, rows] = jnp.sum(squares.T, axis=0, keepdims=True)
        sums_ref[1:2, rows] = jnp.sum(products.T, axis=0, keepdims=True)


def spread(row, width):
    return jnp.broadcast_to(row, (width, row.shape[1])).T


def grad_kernel(sizes, features, *refs):
    heads, length, levels, block, bits = sizes
    attn_ref, gg_ref, qd_ref, tw_ref = refs[:4]
    sums = refs[4:-4]
    ag_ref, inverse_ref, state_ref, scaled_ref = refs[-4:]
    width = attn_ref.shape[-1]
    total = sums[0][...]
    for part in sums[1:]:
        total = total + part[...]
    inverse = lax.rsqrt(total[0:1] / features + epsilon)
    beta = inverse * inverse * inverse * (total[1:2] / features)
    inverse_ref[...] = inverse
    for i in range(length // block):
        rows = slice(i * block, (i + 1) * block)
        left = spread(inverse[:, rows], width)
        right = spread(beta[:, rows], width)
        for head in range(heads):
            grad = (left * gg_ref[head, rows, :] - attn_ref[head, rows, :] * right).astype(BF16)
            ag_ref[head, rows, :] = grad
            wide = grad.astype(F32)
            for j in range(bits):
                at = head * levels + levels - bits + j
                scaled_ref[head, rows, j * width:(j + 1) * width] = (tw_ref[rows, at:at + 1] * wide).astype(BF16)
    for head in range(heads):
        product = dot(qd_ref[head], scaled_ref[head], TN)
        for j in range(bits):
            state_ref[j, head] = product[:, j * width:(j + 1) * width]


def local_backward(sizes, ag_ref, qd_ref, kd_ref, vd_ref, p_ref, w_ref, tw_ref, held_ref, attn_ref,
                   inverse_ref, gain_ref, normed_ref, dq_ref, dk_ref, dv_ref, weighted_ref):
    heads, length, levels, block, bits = sizes
    base = block.bit_length() - 1
    width = ag_ref.shape[-1]
    blocks = length // block
    for i in range(blocks):
        rows = slice(i * block, (i + 1) * block)
        reach = slice(0, (i + 1) * block)
        left = spread(inverse_ref[:, rows], width)
        for head in range(heads):
            put = pl.ds(i * block * heads + head, block, stride=heads)
            normed_ref[put, :] = attn_ref[head, rows, :] * left * gain_ref[head:head + 1, :]
            def weight(level):
                at = head * levels + level
                return tw_ref[rows, at:at + 1]
            grad = ag_ref[head, rows, :]
            scores = dot(grad, vd_ref[head, reach, :], NT)
            for j in range(i + 1):
                part = scores[:, j * block:(j + 1) * block]
                if j == i:
                    part = part * w_ref[head * blocks + i]
                else:
                    part = part * weight(base + (i ^ j).bit_length())
                weighted_ref[head, rows, j * block:(j + 1) * block] = part.astype(BF16)
            total = dot(weighted_ref[head, rows, reach], kd_ref[head, reach, :], NN)
            for j in range(bits):
                total = total + weight(levels - bits + j) * dot(grad, held_ref[j, head], NT)
            dq_ref[put, :] = total
    for head in range(heads):
        for j in range(blocks):
            cols = slice(j * block, (j + 1) * block)
            rest = slice(j * block, length)
            dk_ref[head, cols, :] = dot(weighted_ref[head, rest, cols], qd_ref[head, rest, :], TN)
            dv_ref[head, cols, :] = dot(p_ref[head, rest, cols], ag_ref[head, rest, :], TN)


def final_kernel(sizes, core_ref, near_ref, mine_ref, other_ref, kd_ref, vd_ref, dk_ref, dv_ref,
                 key_ref, value_ref, back_ref):
    heads, length, block = sizes
    join(core_ref, mine_ref, other_ref, back_ref, 0)
    keep = (1 - core_ref[0]).astype(F32)
    for head in range(heads):
        back = (back_ref[head] + keep * near_ref[head]).astype(BF16)
        for i in range(length // block):
            rows = slice(i * block, (i + 1) * block)
            put = pl.ds(i * block * heads + head, block, stride=heads)
            key_ref[put, :] = dk_ref[head, rows, :] + dot(vd_ref[head, rows, :], back, NT)
            value_ref[put, :] = dv_ref[head, rows, :] + dot(kd_ref[head, rows, :], back, NN)


def shards(query_rows, key_rows, value_rows, level_pick, level_table, norm_gain, out_grad):
    length, heads, width = query_rows.shape
    groups, _, levels = level_table.shape
    local_bits = length.bit_length() - 1
    bits = lax.axis_size("seq").bit_length() - 1
    block = min(128, length)
    half = heads // 2
    scale = width ** (-0.5)
    position = lax.axis_index("seq")
    core = position & 1
    core_arg = core.reshape(1).astype(jnp.int32)
    shape = jax.ShapeDtypeStruct

    flags = (position >> jnp.arange(bits, dtype=jnp.int32) & 1).astype(F32)
    factor = scale * jnp.concatenate([jnp.ones((local_bits + 1,), F32), flags])
    table = (level_table * factor[None, None, :]).reshape(groups, heads * levels)
    one_hot = (level_pick[:, None] == jnp.arange(groups, dtype=jnp.int32)[None, :]).astype(F32)
    weights = jnp.dot(one_hot, table, precision=exact_mode)

    own = jnp.einsum("shd,she->hde", key_rows, value_rows, preferred_element_type=F32)
    near = swapped(own, "seq", 0)
    pair = own + near

    def pick(array, which):
        return lax.dynamic_slice_in_dim(array, which * half, half, array.ndim - 3)

    block_sum = pick(pair, core)
    halves = []
    for place in range(1, bits):
        partner = swapped(block_sum, "seq", place)
        halves += [partner, swapped(partner, "seq", 0)]
        block_sum = block_sum + partner

    rows = length * heads
    flat = lambda a: a.reshape(rows, width)
    local_flops = heads * length * length * width
    inner, probs, diag, qd, kd, vd, gg = call(
        functools.partial(local_forward, (heads, length, levels, block)),
        (
            shape((heads, length, width), F32),
            shape((heads, length, length), BF16),
            shape((heads * (length // block), block, block), F32),
            shape((heads, length, width), BF16),
            shape((heads, length, width), BF16),
            shape((heads, length, width), BF16),
            shape((heads, length, width), F32),
        ),
        (flat(query_rows), flat(key_rows), flat(value_rows), flat(out_grad), weights, norm_gain),
        [VMEM] * 6,
        [pltpu.VMEM((rows, width), F32)],
        flops=4 * local_flops,
        name="local_forward",
    )
    sizes = (heads, length, levels, block, bits)
    attn, sums, held = call(
        functools.partial(cross_kernel, sizes),
        (
            shape((heads, length, width), F32),
            shape((2, length), F32),
            shape((bits, heads, width, width), BF16),
        ),
        (core_arg, inner, qd, gg, weights, near, *halves),
        [SMEM] + [VMEM] * (5 + len(halves)),
        flops=2 * bits * heads * length * width * width,
        name="cross",
    )
    features = heads * width * lax.axis_size("heads")
    parts = summands(sums, "heads")
    attn_grad, inverse, grads = call(
        functools.partial(grad_kernel, sizes, features),
        (
            shape((heads, length, width), BF16),
            shape((1, length), F32),
            shape((bits, heads, width, width), F32),
        ),
        (attn, gg, qd, weights, *parts),
        [VMEM] * (4 + len(parts)),
        [pltpu.VMEM((heads, length, bits * width), BF16)],
        flops=2 * bits * heads * length * width * width,
        name="state_grads",
    )
    upper = grads[1:]
    gathered = pick(upper, core) + swapped(pick(upper, 1 - core), "seq", 0)
    back_near = swapped(grads[0], "seq", 0)
    total = jnp.zeros((half, width, width), F32)
    for place in reversed(range(1, bits)):
        total = total + swapped(total + gathered[place - 1], "seq", place)
    other = swapped(total, "seq", 0)

    normed, query_grad, key_part, value_part = call(
        functools.partial(local_backward, sizes),
        (
            shape((rows, width), F32),
            shape((rows, width), F32),
            shape((heads, length, width), F32),
            shape((heads, length, width), F32),
        ),
        (attn_grad, qd, kd, vd, probs, diag, weights, held, attn, inverse, norm_gain),
        [VMEM] * 11,
        [pltpu.VMEM((heads, length, length), BF16)],
        flops=8 * local_flops,
        name="local_backward",
    )
    key_grad, value_grad = call(
        functools.partial(final_kernel, (heads, length, block)),
        (shape((rows, width), F32), shape((rows, width), F32)),
        (core_arg, back_near, total, other, kd, vd, key_part, value_part),
        [SMEM] + [VMEM] * 7,
        [pltpu.VMEM((heads, width, width), F32)],
        flops=4 * heads * length * width * width,
        name="key_value_grads",
    )
    return tuple(a.reshape(length, heads, width) for a in (normed, query_grad, key_grad, value_grad))


def solution(mesh):
    in_specs = (
        P("seq", "heads", None),
        P("seq", "heads", None),
        P("seq", "heads", None),
        P("seq"),
        P(None, "heads", None),
        P("heads", None),
        P("seq", "heads", None),
    )
    out_specs = (
        P("seq", "heads", None),
        P("seq", "heads", None),
        P("seq", "heads", None),
        P("seq", "heads", None),
    )
    return jax.shard_map(shards, mesh=mesh, in_specs=in_specs, out_specs=out_specs, check_vma=False)
```

```python
import functools

import jax
import jax.numpy as jnp
from jax import lax
from jax.experimental import pallas as pl
from jax.experimental.pallas import tpu as pltpu
from jax.sharding import PartitionSpec as P

exact_mode = lax.Precision.HIGHEST
epsilon = 1e-06
F32 = jnp.float32
BF16 = jnp.bfloat16
VMEM = pl.BlockSpec(memory_space=pltpu.VMEM)
HBM = pl.BlockSpec(memory_space=pltpu.HBM)
SMEM = pl.BlockSpec(memory_space=pltpu.SMEM)
NT = (((1,), (1,)), ((), ()))
TN = (((0,), (0,)), ((), ()))
NN = (((1,), (0,)), ((), ()))


def dot(left, right, dims):
    return lax.dot_general(left, right, dims, preferred_element_type=F32)


def swapped(block, axis, distance):
    count = lax.axis_size(axis)
    route = []
    for low in range(count):
        high = low | 1 << distance
        if high != low and high < count:
            route += [(low, high), (high, low)]
    return lax.ppermute(block, axis, route)


def exchanged(block, axis, distance):
    count = lax.axis_size(axis)
    needed, rest = [], []
    for low in range(count):
        high = low | 1 << distance
        if high == low:
            continue
        last = low >> (distance + 1) == (count - 1) >> (distance + 1)
        route = rest if last else needed
        route += [(low, high), (high, low)]
    return [lax.ppermute(block, axis, route) for route in (needed, rest) if route]


def summands(block, axis):
    count = lax.axis_size(axis)
    result = [block]
    for step in range(1, count):
        if count & (count - 1) == 0:
            route = [(i, i ^ step) for i in range(count)]
        else:
            route = [(i, (i + step) % count) for i in range(count)]
        result.append(lax.ppermute(block, axis, route))
    return result


def call(kernel, out_shape, args, specs, scratch=(), flops=0, name=None):
    return pl.pallas_call(
        kernel,
        out_shape=out_shape,
        in_specs=specs,
        out_specs=jax.tree.map(lambda _: VMEM, out_shape),
        scratch_shapes=list(scratch),
        compiler_params=pltpu.CompilerParams(vmem_limit_bytes=16 << 20),
        cost_estimate=pl.CostEstimate(
            flops=flops,
            transcendentals=0,
            bytes_accessed=sum(a.size * a.dtype.itemsize for a in args),
        ),
        name=name,
    )(*args)


def split_heads(source, wide, heads, length, store):
    wide[...] = source[...].astype(F32)
    for head in range(heads):
        store(head, wide[pl.ds(head, length, stride=heads), :])


def level_rows(sizes, scale, position_ref, pick_ref, table_ref, tw_ref):
    heads, length, levels, block, bits = sizes
    groups = table_ref.shape[0]
    lane = lax.broadcasted_iota(jnp.int32, (groups, levels), 1)
    factor = jnp.full((groups, levels), scale, F32)
    for j in range(bits):
        flag = (position_ref[0] >> j & 1).astype(F32) * scale
        factor = jnp.where(lane == levels - bits + j, flag, factor)
    group = lax.broadcasted_iota(jnp.int32, (groups, length), 0)
    one_hot = (group == pick_ref[...]).astype(F32)
    for head in range(heads):
        table = table_ref[:, head, :] * factor
        tw_ref[head] = lax.dot_general(one_hot, table, TN, precision=exact_mode, preferred_element_type=F32)


def local_forward(sizes, scale, position_ref, q_ref, k_ref, v_ref, g_ref, gain_hbm, pick_ref, table_ref,
                  inner_ref, p_ref, w_ref, qd_ref, kd_ref, vd_ref, gg_ref, tw_ref, wide, raw, gain_ref, sems):
    heads, length, levels, block, bits = sizes
    base = block.bit_length() - 1
    copies = [pltpu.make_async_copy(gain_hbm, gain_ref, sems.at[4])]
    for n, source in enumerate((k_ref, v_ref, q_ref, g_ref)):
        copies.append(pltpu.make_async_copy(source, raw.at[n], sems.at[n]))
    for copy in copies:
        copy.start()
    level_rows(sizes, scale, position_ref, pick_ref, table_ref, tw_ref)
    for n, target in enumerate((kd_ref, vd_ref, qd_ref)):
        def store(head, value, target=target):
            target[head] = value.astype(BF16)
        copies[n + 1].wait()
        split_heads(raw.at[n], wide, heads, length, store)
    copies[4].wait()
    copies[0].wait()

    def store_gain(head, value):
        gg_ref[head] = value * gain_ref[head:head + 1, :]
    split_heads(raw.at[3], wide, heads, length, store_gain)
    row = lax.broadcasted_iota(jnp.int32, (block, block), 0)
    column = lax.broadcasted_iota(jnp.int32, (block, block), 1)
    differs = row ^ column
    below = column <= row
    for head in range(heads):
        for i in range(length // block):
            rows = slice(i * block, (i + 1) * block)
            reach = slice(0, (i + 1) * block)
            def weight(level):
                return tw_ref[head, rows, level:level + 1]
            diagonal = jnp.broadcast_to(weight(0), (block, block))
            for level in range(1, base + 1):
                diagonal = jnp.where(differs >= 1 << (level - 1), weight(level), diagonal)
            diagonal = jnp.where(below, diagonal, 0.0)
            w_ref[head * (length // block) + i] = diagonal
            scores = dot(qd_ref[head, rows, :], kd_ref[head, reach, :], NT)
            parts = []
            for j in range(i):
                parts.append(scores[:, j * block:(j + 1) * block] * weight(base + (i ^ j).bit_length()))
            parts.append(scores[:, rows] * diagonal)
            for j, part in enumerate(parts):
                p_ref[head, rows, j * block:(j + 1) * block] = part.astype(BF16)
            inner_ref[head, rows, :] = dot(p_ref[head, rows, reach], vd_ref[head, reach, :], NN)


def join(core_ref, mine_ref, other_ref, target_ref, first, lead=None):
    half = mine_ref.shape[-3]
    core = (core_ref[0] & 1)
    for h in range(half):
        for source, start in ((mine_ref, core * half), (other_ref, (1 - core) * half)):
            if lead is None:
                target_ref[start + h] = source[h].astype(target_ref.dtype)
            else:
                target_ref[first, start + h] = source[h].astype(target_ref.dtype)


def cross_kernel(sizes, *refs):
    heads, length, levels, block, bits = sizes
    core_ref, inner_ref, qd_ref, gg_ref, tw_ref, near_ref = refs[:6]
    halves = refs[6:6 + 2 * (bits - 1)]
    attn_ref, sums_ref, held_ref = refs[-3:]
    held_ref[0] = near_ref[...].astype(BF16)
    for j in range(1, bits):
        join(core_ref, halves[2 * j - 2], halves[2 * j - 1], held_ref, j, lead=True)
    for i in range(length // block):
        rows = slice(i * block, (i + 1) * block)
        squares = 0.0
        products = 0.0
        for head in range(heads):
            total = inner_ref[head, rows, :]
            query = qd_ref[head, rows, :]
            for j in range(bits):
                at = levels - bits + j
                total = total + tw_ref[head, rows, at:at + 1] * dot(query, held_ref[j, head], NN)
            attn_ref[head, rows, :] = total
            squares = squares + total * total
            products = products + total * gg_ref[head, rows, :]
        sums_ref[0:1, rows] = jnp.sum(squares.T, axis=0, keepdims=True)
        sums_ref[1:2, rows] = jnp.sum(products.T, axis=0, keepdims=True)


def spread(row, width):
    return jnp.broadcast_to(row, (width, row.shape[1])).T


def grad_kernel(sizes, features, *refs):
    heads, length, levels, block, bits = sizes
    position_ref, attn_ref, gg_ref, qd_ref, tw_ref = refs[:5]
    sums = refs[5:-7]
    ag_ref, inverse_ref, first_ref, keep_ref, send_ref, scaled_ref, state_ref = refs[-7:]
    width = attn_ref.shape[-1]
    total = sums[0][...]
    for part in sums[1:]:
        total = total + part[...]
    inverse = lax.rsqrt(total[0:1] / features + epsilon)
    beta = inverse * inverse * inverse * (total[1:2] / features)
    inverse_ref[...] = inverse
    for i in range(length // block):
        rows = slice(i * block, (i + 1) * block)
        left = spread(inverse[:, rows], width)
        right = spread(beta[:, rows], width)
        for head in range(heads):
            grad = (left * gg_ref[head, rows, :] - attn_ref[head, rows, :] * right).astype(BF16)
            ag_ref[head, rows, :] = grad
            wide = grad.astype(F32)
            for j in range(bits):
                at = levels - bits + j
                scaled_ref[head, rows, j * width:(j + 1) * width] = (tw_ref[head, rows, at:at + 1] * wide).astype(BF16)
    for head in range(heads):
        product = dot(qd_ref[head], scaled_ref[head], TN)
        first_ref[head] = product[:, :width]
        for j in range(1, bits):
            state_ref[j - 1, head] = product[:, j * width:(j + 1) * width]
    half = heads // 2
    core = position_ref[0] & 1
    for j in range(bits - 1):
        for h in range(half):
            keep_ref[j, h] = state_ref[j, core * half + h]
            send_ref[j, h] = state_ref[j, (1 - core) * half + h]


def local_backward(sizes, ag_ref, qd_ref, kd_ref, vd_ref, p_ref, w_ref, tw_ref, held_ref, attn_ref,
                   inverse_ref, gain_ref, normed_ref, dq_ref, dk_ref, dv_ref, weighted_ref):
    heads, length, levels, block, bits = sizes
    base = block.bit_length() - 1
    width = ag_ref.shape[-1]
    blocks = length // block
    for i in range(blocks):
        rows = slice(i * block, (i + 1) * block)
        reach = slice(0, (i + 1) * block)
        left = spread(inverse_ref[:, rows], width)
        for head in range(heads):
            put = pl.ds(i * block * heads + head, block, stride=heads)
            normed_ref[put, :] = attn_ref[head, rows, :] * left * gain_ref[head:head + 1, :]
            def weight(level):
                return tw_ref[head, rows, level:level + 1]
            grad = ag_ref[head, rows, :]
            scores = dot(grad, vd_ref[head, reach, :], NT)
            for j in range(i + 1):
                part = scores[:, j * block:(j + 1) * block]
                if j == i:
                    part = part * w_ref[head * blocks + i]
                else:
                    part = part * weight(base + (i ^ j).bit_length())
                weighted_ref[head, rows, j * block:(j + 1) * block] = part.astype(BF16)
            total = dot(weighted_ref[head, rows, reach], kd_ref[head, reach, :], NN)
            for j in range(bits):
                total = total + weight(levels - bits + j) * dot(grad, held_ref[j, head], NT)
            dq_ref[put, :] = total
    for head in range(heads):
        for j in range(blocks):
            cols = slice(j * block, (j + 1) * block)
            rest = slice(j * block, length)
            dk_ref[head, cols, :] = dot(weighted_ref[head, rest, cols], qd_ref[head, rest, :], TN)
            dv_ref[head, cols, :] = dot(p_ref[head, rest, cols], ag_ref[head, rest, :], TN)


def final_kernel(sizes, core_ref, near_ref, mine_ref, other_ref, kd_ref, vd_ref, dk_ref, dv_ref,
                 key_ref, value_ref, back_ref):
    heads, length, block = sizes
    join(core_ref, mine_ref, other_ref, back_ref, 0)
    keep = (1 - (core_ref[0] & 1)).astype(F32)
    for head in range(heads):
        back = (back_ref[head] + keep * near_ref[head]).astype(BF16)
        for i in range(length // block):
            rows = slice(i * block, (i + 1) * block)
            put = pl.ds(i * block * heads + head, block, stride=heads)
            key_ref[put, :] = dk_ref[head, rows, :] + dot(vd_ref[head, rows, :], back, NT)
            value_ref[put, :] = dv_ref[head, rows, :] + dot(kd_ref[head, rows, :], back, NN)


def shards(query_rows, key_rows, value_rows, level_pick, level_table, norm_gain, out_grad):
    length, heads, width = query_rows.shape
    groups, _, levels = level_table.shape
    local_bits = length.bit_length() - 1
    bits = lax.axis_size("seq").bit_length() - 1
    block = min(128, length)
    half = heads // 2
    scale = width ** (-0.5)
    position = lax.axis_index("seq").astype(jnp.int32)
    place_arg = position.reshape(1)
    shape = jax.ShapeDtypeStruct

    own = jnp.einsum("shd,she->hde", key_rows, value_rows, preferred_element_type=F32)
    near = swapped(own, "seq", 0)
    pair = own + near

    block_sum = lax.dynamic_slice(
        pair, ((position & 1) * half, 0, 0), (half, width, width), allow_negative_indices=False
    )
    partners = []
    for place in range(1, bits):
        arrived = exchanged(block_sum, "seq", place)
        partners.append(arrived)
        block_sum = block_sum + arrived[0]

    rows = length * heads
    flat = lambda a: a.reshape(rows, width)
    local_flops = heads * length * length * width
    sizes = (heads, length, levels, block, bits)
    inner, probs, diag, qd, kd, vd, gg, weights = call(
        functools.partial(local_forward, sizes, scale),
        (
            shape((heads, length, width), F32),
            shape((heads, length, length), BF16),
            shape((heads * (length // block), block, block), F32),
            shape((heads, length, width), BF16),
            shape((heads, length, width), BF16),
            shape((heads, length, width), BF16),
            shape((heads, length, width), F32),
            shape((heads, length, levels), F32),
        ),
        (
            place_arg,
            flat(query_rows),
            flat(key_rows),
            flat(value_rows),
            flat(out_grad),
            norm_gain,
            level_pick.reshape(1, length),
            level_table,
        ),
        [SMEM, HBM, HBM, HBM, HBM, HBM, VMEM, VMEM],
        [
            pltpu.VMEM((rows, width), F32),
            pltpu.VMEM((4, rows, width), BF16),
            pltpu.VMEM((heads, width), F32),
            pltpu.SemaphoreType.DMA((5,)),
        ],
        flops=4 * local_flops,
        name="local_forward",
    )
    inner, partners = lax.optimization_barrier((inner, partners))
    halves = []
    for arrived in partners:
        partner = functools.reduce(jnp.add, arrived)
        halves += [partner, swapped(partner, "seq", 0)]
    attn, sums, held = call(
        functools.partial(cross_kernel, sizes),
        (
            shape((heads, length, width), F32),
            shape((2, length), F32),
            shape((bits, heads, width, width), BF16),
        ),
        (place_arg, inner, qd, gg, weights, near, *halves, diag),
        [SMEM] + [VMEM] * (6 + len(halves)),
        flops=2 * bits * heads * length * width * width,
        name="cross",
    )
    features = heads * width * lax.axis_size("heads")
    parts = summands(sums, "heads")
    attn_grad, inverse, first, keep, send = call(
        functools.partial(grad_kernel, sizes, features),
        (
            shape((heads, length, width), BF16),
            shape((1, length), F32),
            shape((heads, width, width), F32),
            shape((bits - 1, half, width, width), F32),
            shape((bits - 1, half, width, width), F32),
        ),
        (place_arg, attn, gg, qd, weights, *parts),
        [SMEM] + [VMEM] * (4 + len(parts)),
        [
            pltpu.VMEM((heads, length, bits * width), BF16),
            pltpu.VMEM((bits - 1, heads, width, width), F32),
        ],
        flops=2 * bits * heads * length * width * width,
        name="state_grads",
    )
    gathered = keep + swapped(send, "seq", 0)
    back_near = swapped(first, "seq", 0)

    normed, query_grad, key_part, value_part = call(
        functools.partial(local_backward, sizes),
        (
            shape((rows, width), F32),
            shape((rows, width), F32),
            shape((heads, length, width), F32),
            shape((heads, length, width), F32),
        ),
        (attn_grad, qd, kd, vd, probs, diag, weights, held, attn, inverse, norm_gain),
        [VMEM] * 11,
        [pltpu.VMEM((heads, length, length), BF16)],
        flops=8 * local_flops,
        name="local_backward",
    )
    total = jnp.zeros((half, width, width), F32)
    for place in reversed(range(1, bits)):
        total = total + swapped(total + gathered[place - 1], "seq", place)
        if place == bits - 1:
            total, key_part = lax.optimization_barrier((total, key_part))
    other = swapped(total, "seq", 0)

    key_grad, value_grad = call(
        functools.partial(final_kernel, (heads, length, block)),
        (shape((rows, width), F32), shape((rows, width), F32)),
        (place_arg, back_near, total, other, kd, vd, key_part, value_part),
        [SMEM] + [VMEM] * 7,
        [pltpu.VMEM((heads, width, width), F32)],
        flops=4 * heads * length * width * width,
        name="key_value_grads",
    )
    return tuple(a.reshape(length, heads, width) for a in (normed, query_grad, key_grad, value_grad))


def solution(mesh):
    in_specs = (
        P("seq", "heads", None),
        P("seq", "heads", None),
        P("seq", "heads", None),
        P("seq"),
        P(None, "heads", None),
        P("heads", None),
        P("seq", "heads", None),
    )
    out_specs = (
        P("seq", "heads", None),
        P("seq", "heads", None),
        P("seq", "heads", None),
        P("seq", "heads", None),
    )
    return jax.shard_map(shards, mesh=mesh, in_specs=in_specs, out_specs=out_specs, check_vma=False)
```

```python
import functools

import jax
import jax.numpy as jnp
from jax import lax
from jax.experimental import pallas as pl
from jax.experimental.pallas import tpu as pltpu
from jax.sharding import PartitionSpec as P

exact_mode = lax.Precision.HIGHEST
epsilon = 1e-06
F32 = jnp.float32
BF16 = jnp.bfloat16
VMEM = pl.BlockSpec(memory_space=pltpu.VMEM)
HBM = pl.BlockSpec(memory_space=pltpu.HBM)
SMEM = pl.BlockSpec(memory_space=pltpu.SMEM)
NT = (((1,), (1,)), ((), ()))
TN = (((0,), (0,)), ((), ()))
NN = (((1,), (0,)), ((), ()))


def dot(left, right, dims):
    return lax.dot_general(left, right, dims, preferred_element_type=F32)


def swapped(block, axis, distance):
    count = lax.axis_size(axis)
    route = []
    for low in range(count):
        high = low | 1 << distance
        if high != low and high < count:
            route += [(low, high), (high, low)]
    return lax.ppermute(block, axis, route)


def exchanged(block, axis, distance):
    count = lax.axis_size(axis)
    needed, rest = [], []
    for low in range(count):
        high = low | 1 << distance
        if high == low:
            continue
        last = low >> (distance + 1) == (count - 1) >> (distance + 1)
        route = rest if last else needed
        route += [(low, high), (high, low)]
    return [lax.ppermute(block, axis, route) for route in (needed, rest) if route]


def summands(block, axis):
    count = lax.axis_size(axis)
    result = [block]
    for step in range(1, count):
        if count & (count - 1) == 0:
            route = [(i, i ^ step) for i in range(count)]
        else:
            route = [(i, (i + step) % count) for i in range(count)]
        result.append(lax.ppermute(block, axis, route))
    return result


def call(kernel, out_shape, args, specs, scratch=(), flops=0, name=None, outs=VMEM):
    return pl.pallas_call(
        kernel,
        out_shape=out_shape,
        in_specs=specs,
        out_specs=jax.tree.map(lambda _: outs, out_shape),
        scratch_shapes=list(scratch),
        compiler_params=pltpu.CompilerParams(vmem_limit_bytes=16 << 20),
        cost_estimate=pl.CostEstimate(
            flops=flops,
            transcendentals=0,
            bytes_accessed=sum(a.size * a.dtype.itemsize for a in args),
        ),
        name=name,
    )(*args)


def split_heads(source, wide, heads, length, store):
    wide[...] = source[...].astype(F32)
    for head in range(heads):
        store(head, wide[pl.ds(head, length, stride=heads), :])


def level_rows(sizes, scale, position_ref, pick_ref, table_ref, tw_ref):
    heads, length, levels, block, bits = sizes
    groups = table_ref.shape[0]
    lane = lax.broadcasted_iota(jnp.int32, (groups, levels), 1)
    factor = jnp.full((groups, levels), scale, F32)
    for j in range(bits):
        flag = (position_ref[0] >> j & 1).astype(F32) * scale
        factor = jnp.where(lane == levels - bits + j, flag, factor)
    group = lax.broadcasted_iota(jnp.int32, (groups, length), 0)
    one_hot = (group == pick_ref[...]).astype(F32)
    for head in range(heads):
        table = table_ref[:, head, :] * factor
        tw_ref[head] = lax.dot_general(one_hot, table, TN, precision=exact_mode, preferred_element_type=F32)


def local_forward(sizes, scale, position_ref, q_ref, k_ref, v_ref, g_ref, gain_hbm, pick_ref, table_ref,
                  inner_ref, p_ref, w_ref, qd_ref, kd_ref, vd_ref, gg_ref, tw_ref, wide, raw, gain_ref, sems):
    heads, length, levels, block, bits = sizes
    base = block.bit_length() - 1
    copies = [pltpu.make_async_copy(gain_hbm, gain_ref, sems.at[4])]
    for n, source in enumerate((k_ref, v_ref, q_ref, g_ref)):
        copies.append(pltpu.make_async_copy(source, raw.at[n], sems.at[n]))
    for copy in copies:
        copy.start()
    level_rows(sizes, scale, position_ref, pick_ref, table_ref, tw_ref)
    for n, target in enumerate((kd_ref, vd_ref, qd_ref)):
        def store(head, value, target=target):
            target[head] = value.astype(BF16)
        copies[n + 1].wait()
        split_heads(raw.at[n], wide, heads, length, store)
    copies[4].wait()
    copies[0].wait()

    def store_gain(head, value):
        gg_ref[head] = value * gain_ref[head:head + 1, :]
    split_heads(raw.at[3], wide, heads, length, store_gain)
    row = lax.broadcasted_iota(jnp.int32, (block, block), 0)
    column = lax.broadcasted_iota(jnp.int32, (block, block), 1)
    differs = row ^ column
    below = column <= row
    for head in range(heads):
        for i in range(length // block):
            rows = slice(i * block, (i + 1) * block)
            reach = slice(0, (i + 1) * block)
            def weight(level):
                return tw_ref[head, rows, level:level + 1]
            diagonal = jnp.broadcast_to(weight(0), (block, block))
            for level in range(1, base + 1):
                diagonal = jnp.where(differs >= 1 << (level - 1), weight(level), diagonal)
            diagonal = jnp.where(below, diagonal, 0.0)
            w_ref[head * (length // block) + i] = diagonal
            scores = dot(qd_ref[head, rows, :], kd_ref[head, reach, :], NT)
            parts = []
            for j in range(i):
                parts.append(scores[:, j * block:(j + 1) * block] * weight(base + (i ^ j).bit_length()))
            parts.append(scores[:, rows] * diagonal)
            for j, part in enumerate(parts):
                p_ref[head, rows, j * block:(j + 1) * block] = part.astype(BF16)
            inner_ref[head, rows, :] = dot(p_ref[head, rows, reach], vd_ref[head, reach, :], NN)


def cross_heads(sizes, heads_at, held_at, inner_ref, qd_ref, gg_ref, tw_ref, attn_ref, sums_ref, add=None):
    _, length, levels, block, bits = sizes
    for i in range(length // block):
        rows = slice(i * block, (i + 1) * block)
        squares = 0.0
        products = 0.0
        for h, head in enumerate(heads_at):
            total = inner_ref[head, rows, :]
            query = qd_ref[head, rows, :]
            for j in range(bits):
                at = levels - bits + j
                total = total + tw_ref[head, rows, at:at + 1] * dot(query, held_at(j, h), NN)
            attn_ref[h, rows, :] = total
            squares = squares + total * total
            products = products + total * gg_ref[head, rows, :]
        both = (squares, products)
        for n in range(2):
            row = jnp.sum(both[n].T, axis=0, keepdims=True)
            if add is not None:
                row = row + add[n:n + 1, rows]
            sums_ref[n:n + 1, rows] = row


def cross_mine(sizes, *refs):
    heads, length, levels, block, bits = sizes
    position_ref, inner_ref, qd_ref, gg_ref, tw_ref, near_ref = refs[:6]
    mine = refs[6:6 + bits - 1]
    attn_ref, sums_ref, held_ref = refs[-3:]
    half = heads // 2
    start = (position_ref[0] & 1) * half
    for h in range(half):
        held_ref[0, h] = near_ref[start + h].astype(BF16)
        for j in range(1, bits):
            held_ref[j, h] = mine[j - 1][h].astype(BF16)
    cross_heads(sizes, [start + h for h in range(half)], lambda j, h: held_ref[j, h],
                inner_ref, qd_ref, gg_ref, tw_ref, attn_ref, sums_ref)


def cross_other(sizes, *refs):
    heads, length, levels, block, bits = sizes
    position_ref, inner_ref, qd_ref, gg_ref, tw_ref, near_ref, add_ref = refs[:7]
    other = refs[7:7 + bits - 1]
    attn_ref, sums_ref, held_ref = refs[-3:]
    half = heads // 2
    start = (1 - (position_ref[0] & 1)) * half
    for h in range(half):
        held_ref[0, h] = near_ref[start + h].astype(BF16)
        for j in range(1, bits):
            held_ref[j, h] = other[j - 1][h].astype(BF16)
    cross_heads(sizes, [start + h for h in range(half)], lambda j, h: held_ref[j, h],
                inner_ref, qd_ref, gg_ref, tw_ref, attn_ref, sums_ref, add_ref)


def spread(row, width):
    return jnp.broadcast_to(row, (width, row.shape[1])).T


def token_scales(features, sums):
    total = sums[0][...]
    for part in sums[1:]:
        total = total + part[...]
    inverse = lax.rsqrt(total[0:1] / features + epsilon)
    return inverse, inverse * inverse * inverse * (total[1:2] / features)


def grad_heads(sizes, heads_at, left_at, right_at, attn_ref, gg_ref, qd_ref, tw_ref, put_grad, scaled_ref, put_state):
    _, length, levels, block, bits = sizes
    width = attn_ref.shape[-1]
    for h, head in enumerate(heads_at):
        for i in range(length // block):
            rows = slice(i * block, (i + 1) * block)
            grad = (left_at(rows) * gg_ref[head, rows, :] - attn_ref[h, rows, :] * right_at(rows)).astype(BF16)
            put_grad(h, rows, grad)
            wide = grad.astype(F32)
            for j in range(bits):
                at = levels - bits + j
                scaled_ref[rows, j * width:(j + 1) * width] = (tw_ref[head, rows, at:at + 1] * wide).astype(BF16)
        product = dot(qd_ref[head], scaled_ref[...], TN)
        for j in range(bits):
            put_state(j, h, product[:, j * width:(j + 1) * width])


def grad_other(sizes, features, *refs):
    heads, length, levels, block, bits = sizes
    position_ref, attn_ref, gg_ref, qd_ref, tw_ref = refs[:5]
    sums = refs[5:-7]
    ag_ref, inverse_ref, left_ref, right_ref, first_ref, send_ref, scaled_ref = refs[-7:]
    half = heads // 2
    start = (1 - (position_ref[0] & 1)) * half
    width = attn_ref.shape[-1]
    inverse, beta = token_scales(features, sums)
    inverse_ref[...] = inverse
    for i in range(length // block):
        rows = slice(i * block, (i + 1) * block)
        left_ref[rows, :] = spread(inverse[:, rows], width)
        right_ref[rows, :] = spread(beta[:, rows], width)

    def put_grad(h, rows, grad):
        ag_ref[h, rows, :] = grad

    def put_state(j, h, value):
        if j == 0:
            first_ref[h] = value
        else:
            send_ref[j - 1, h] = value
    grad_heads(sizes, [start + h for h in range(half)], lambda rows: left_ref[rows, :], lambda rows: right_ref[rows, :],
               attn_ref, gg_ref, qd_ref, tw_ref, put_grad, scaled_ref, put_state)


def grad_mine(sizes, position_ref, attn_ref, far_ref, gg_ref, qd_ref, tw_ref, other_ref, left_ref, right_ref,
              held_mine_ref, held_other_ref, ag_ref, first_ref, keep_ref, attn_full_ref, held_ref, scaled_ref):
    heads, length, levels, block, bits = sizes
    half = heads // 2
    core = position_ref[0] & 1
    start = core * half
    away = (1 - core) * half

    def put_grad(h, rows, grad):
        ag_ref[start + h, rows, :] = grad

    def put_state(j, h, value):
        if j == 0:
            first_ref[h] = value
        else:
            keep_ref[j - 1, h] = value
    grad_heads(sizes, [start + h for h in range(half)], lambda rows: left_ref[rows, :], lambda rows: right_ref[rows, :],
               attn_ref, gg_ref, qd_ref, tw_ref, put_grad, scaled_ref, put_state)
    for h in range(half):
        ag_ref[away + h] = other_ref[h]
        attn_full_ref[start + h] = attn_ref[h]
        attn_full_ref[away + h] = far_ref[h]
        for j in range(bits):
            held_ref[j, start + h] = held_mine_ref[j, h]
            held_ref[j, away + h] = held_other_ref[j, h]


def local_backward(sizes, ag_ref, qd_ref, kd_ref, vd_ref, p_ref, w_ref, tw_ref, held_ref, attn_ref,
                   inverse_ref, gain_ref, normed_ref, dq_ref, dk_ref, dv_ref, weighted_ref):
    heads, length, levels, block, bits = sizes
    base = block.bit_length() - 1
    width = ag_ref.shape[-1]
    blocks = length // block
    for i in range(blocks):
        rows = slice(i * block, (i + 1) * block)
        reach = slice(0, (i + 1) * block)
        left = spread(inverse_ref[:, rows], width)
        for head in range(heads):
            put = pl.ds(i * block * heads + head, block, stride=heads)
            normed_ref[put, :] = attn_ref[head, rows, :] * left * gain_ref[head:head + 1, :]
            def weight(level):
                return tw_ref[head, rows, level:level + 1]
            grad = ag_ref[head, rows, :]
            scores = dot(grad, vd_ref[head, reach, :], NT)
            for j in range(i + 1):
                part = scores[:, j * block:(j + 1) * block]
                if j == i:
                    part = part * w_ref[head * blocks + i]
                else:
                    part = part * weight(base + (i ^ j).bit_length())
                weighted_ref[head, rows, j * block:(j + 1) * block] = part.astype(BF16)
            total = dot(weighted_ref[head, rows, reach], kd_ref[head, reach, :], NN)
            for j in range(bits):
                total = total + weight(levels - bits + j) * dot(grad, held_ref[j, head], NT)
            dq_ref[put, :] = total
    for head in range(heads):
        for j in range(blocks):
            cols = slice(j * block, (j + 1) * block)
            rest = slice(j * block, length)
            dk_ref[head, cols, :] = dot(weighted_ref[head, rest, cols], qd_ref[head, rest, :], TN)
            dv_ref[head, cols, :] = dot(p_ref[head, rest, cols], ag_ref[head, rest, :], TN)


def final_mine(sizes, position_ref, near_ref, total_ref, kd_ref, vd_ref, dk_ref, dv_ref, key_ref, value_ref):
    heads, length, block = sizes
    half = heads // 2
    core = position_ref[0] & 1
    keep = (1 - core).astype(F32)
    for h in range(half):
        head = core * half + h
        back = (total_ref[h] + keep * near_ref[h]).astype(BF16)
        key_ref[h] = dk_ref[head] + dot(vd_ref[head], back, NT)
        value_ref[h] = dv_ref[head] + dot(kd_ref[head], back, NN)


def final_other(sizes, position_ref, near_ref, total_ref, kd_ref, vd_ref, dk_ref, dv_ref, mine_key_ref, mine_value_ref,
                key_hbm, value_hbm, back_ref, key_ref, value_ref, sems):
    heads, length, block = sizes
    half = heads // 2
    core = position_ref[0] & 1
    keep = (1 - core).astype(F32)
    away = (1 - core) * half
    for h in range(half):
        back_ref[h] = (total_ref[h] + keep * near_ref[h]).astype(BF16)
    copies = []
    for i in range(length // block):
        rows = slice(i * block, (i + 1) * block)
        new = []
        for h in range(half):
            head = away + h
            back = back_ref[h]
            new.append((dk_ref[head, rows, :] + dot(vd_ref[head, rows, :], back, NT),
                        dv_ref[head, rows, :] + dot(kd_ref[head, rows, :], back, NN)))
        for h in range(half):
            old = (mine_key_ref[h, rows, :], mine_value_ref[h, rows, :])
            for n, target in enumerate((key_ref, value_ref)):
                low = jnp.where(core == 0, old[n], new[h][n])
                high = jnp.where(core == 0, new[h][n], old[n])
                target[pl.ds(i * block * heads + h, block, stride=heads), :] = low
                target[pl.ds(i * block * heads + half + h, block, stride=heads), :] = high
        chunk = pl.ds(i * block * heads, block * heads)
        for n, (source, target) in enumerate(((key_ref, key_hbm), (value_ref, value_hbm))):
            copy = pltpu.make_async_copy(source.at[chunk], target.at[chunk], sems.at[n, i])
            copy.start()
            copies.append(copy)
    for copy in copies:
        copy.wait()


def shards(query_rows, key_rows, value_rows, level_pick, level_table, norm_gain, out_grad):
    length, heads, width = query_rows.shape
    groups, _, levels = level_table.shape
    local_bits = length.bit_length() - 1
    bits = lax.axis_size("seq").bit_length() - 1
    block = min(128, length)
    half = heads // 2
    scale = width ** (-0.5)
    position = lax.axis_index("seq").astype(jnp.int32)
    place_arg = position.reshape(1)
    shape = jax.ShapeDtypeStruct

    own = jnp.einsum("shd,she->hde", key_rows, value_rows, preferred_element_type=F32)
    near = swapped(own, "seq", 0)
    pair = own + near

    block_sum = lax.dynamic_slice(
        pair, ((position & 1) * half, 0, 0), (half, width, width), allow_negative_indices=False
    )
    partners = []
    for place in range(1, bits):
        arrived = exchanged(block_sum, "seq", place)
        partners.append(arrived)
        block_sum = block_sum + arrived[0]

    rows = length * heads
    flat = lambda a: a.reshape(rows, width)
    local_flops = heads * length * length * width
    sizes = (heads, length, levels, block, bits)
    inner, probs, diag, qd, kd, vd, gg, weights = call(
        functools.partial(local_forward, sizes, scale),
        (
            shape((heads, length, width), F32),
            shape((heads, length, length), BF16),
            shape((heads * (length // block), block, block), F32),
            shape((heads, length, width), BF16),
            shape((heads, length, width), BF16),
            shape((heads, length, width), BF16),
            shape((heads, length, width), F32),
            shape((heads, length, levels), F32),
        ),
        (
            place_arg,
            flat(query_rows),
            flat(key_rows),
            flat(value_rows),
            flat(out_grad),
            norm_gain,
            level_pick.reshape(1, length),
            level_table,
        ),
        [SMEM, HBM, HBM, HBM, HBM, HBM, VMEM, VMEM],
        [
            pltpu.VMEM((rows, width), F32),
            pltpu.VMEM((4, rows, width), BF16),
            pltpu.VMEM((heads, width), F32),
            pltpu.SemaphoreType.DMA((5,)),
        ],
        flops=4 * local_flops,
        name="local_forward",
    )
    inner, partners = lax.optimization_barrier((inner, partners))
    mine = [functools.reduce(jnp.add, arrived) for arrived in partners]
    others = [swapped(partner, "seq", 0) for partner in mine]
    cross_flops = bits * heads * length * width * width
    cross_shapes = (
        shape((half, length, width), F32),
        shape((2, length), F32),
        shape((bits, half, width, width), BF16),
    )
    attn_mine, sums, held_mine = call(
        functools.partial(cross_mine, sizes),
        cross_shapes,
        (place_arg, inner, qd, gg, weights, near, *mine),
        [SMEM] + [VMEM] * (5 + len(mine)),
        flops=cross_flops,
        name="cross_mine",
    )
    attn_other, sums, held_other = call(
        functools.partial(cross_other, sizes),
        cross_shapes,
        (place_arg, inner, qd, gg, weights, near, sums, *others),
        [SMEM] + [VMEM] * (6 + len(others)),
        flops=cross_flops,
        name="cross_other",
    )
    features = heads * width * lax.axis_size("heads")
    parts = summands(sums, "heads")
    grad_far, inverse, left, right, first_other, send = call(
        functools.partial(grad_other, sizes, features),
        (
            shape((half, length, width), BF16),
            shape((1, length), F32),
            shape((length, width), F32),
            shape((length, width), F32),
            shape((half, width, width), F32),
            shape((bits - 1, half, width, width), F32),
        ),
        (place_arg, attn_other, gg, qd, weights, *parts),
        [SMEM] + [VMEM] * (4 + len(parts)),
        [pltpu.VMEM((length, bits * width), BF16)],
        flops=cross_flops,
        name="state_grads_other",
    )
    attn_grad, first_mine, keep, attn, held = call(
        functools.partial(grad_mine, sizes),
        (
            shape((heads, length, width), BF16),
            shape((half, width, width), F32),
            shape((bits - 1, half, width, width), F32),
            shape((heads, length, width), F32),
            shape((bits, heads, width, width), BF16),
        ),
        (place_arg, attn_mine, attn_other, gg, qd, weights, grad_far, left, right, held_mine, held_other),
        [SMEM] + [VMEM] * 10,
        [pltpu.VMEM((length, bits * width), BF16)],
        flops=cross_flops,
        name="state_grads_mine",
    )
    gathered = keep + swapped(send, "seq", 0)
    near_other = swapped(first_mine, "seq", 0)
    near_mine = swapped(first_other, "seq", 0)

    normed, query_grad, key_part, value_part = call(
        functools.partial(local_backward, sizes),
        (
            shape((rows, width), F32),
            shape((rows, width), F32),
            shape((heads, length, width), F32),
            shape((heads, length, width), F32),
        ),
        (attn_grad, qd, kd, vd, probs, diag, weights, held, attn, inverse, norm_gain),
        [VMEM] * 11,
        [pltpu.VMEM((heads, length, length), BF16)],
        flops=8 * local_flops,
        name="local_backward",
    )
    total = jnp.zeros((half, width, width), F32)
    for place in reversed(range(1, bits)):
        total = total + swapped(total + gathered[place - 1], "seq", place)
        if place == bits - 1:
            total, key_part = lax.optimization_barrier((total, key_part))
    other = swapped(total, "seq", 0)

    final_sizes = (heads, length, block)
    final_flops = 2 * heads * length * width * width
    key_mine, value_mine = call(
        functools.partial(final_mine, final_sizes),
        (shape((half, length, width), F32), shape((half, length, width), F32)),
        (place_arg, near_mine, total, kd, vd, key_part, value_part),
        [SMEM] + [VMEM] * 6,
        flops=final_flops,
        name="key_value_mine",
    )
    key_grad, value_grad = call(
        functools.partial(final_other, final_sizes),
        (shape((rows, width), F32), shape((rows, width), F32)),
        (place_arg, near_other, other, kd, vd, key_part, value_part, key_mine, value_mine),
        [SMEM] + [VMEM] * 8,
        [
            pltpu.VMEM((half, width, width), BF16),
            pltpu.VMEM((rows, width), F32),
            pltpu.VMEM((rows, width), F32),
            pltpu.SemaphoreType.DMA((2, length // block)),
        ],
        flops=final_flops,
        name="key_value_other",
        outs=HBM,
    )
    return tuple(a.reshape(length, heads, width) for a in (normed, query_grad, key_grad, value_grad))


def solution(mesh):
    in_specs = (
        P("seq", "heads", None),
        P("seq", "heads", None),
        P("seq", "heads", None),
        P("seq"),
        P(None, "heads", None),
        P("heads", None),
        P("seq", "heads", None),
    )
    out_specs = (
        P("seq", "heads", None),
        P("seq", "heads", None),
        P("seq", "heads", None),
        P("seq", "heads", None),
    )
    return jax.shard_map(shards, mesh=mesh, in_specs=in_specs, out_specs=out_specs, check_vma=False)
```

```python
import functools

import jax
import jax.numpy as jnp
from jax import lax
from jax.experimental import pallas as pl
from jax.experimental.pallas import tpu as pltpu
from jax.sharding import PartitionSpec as P

exact_mode = lax.Precision.HIGHEST
epsilon = 1e-06
F32 = jnp.float32
BF16 = jnp.bfloat16
VMEM = pl.BlockSpec(memory_space=pltpu.VMEM)
HBM = pl.BlockSpec(memory_space=pltpu.HBM)
SMEM = pl.BlockSpec(memory_space=pltpu.SMEM)
NT = (((1,), (1,)), ((), ()))
TN = (((0,), (0,)), ((), ()))
NN = (((1,), (0,)), ((), ()))


def dot(left, right, dims):
    return lax.dot_general(left, right, dims, preferred_element_type=F32)


def swapped(block, axis, distance):
    count = lax.axis_size(axis)
    route = []
    for low in range(count):
        high = low | 1 << distance
        if high != low and high < count:
            route += [(low, high), (high, low)]
    return lax.ppermute(block, axis, route)


def turns(count):
    order = []
    for step in range(1, count // 2 + 1):
        order += [step] if 2 * step == count else [step, count - step]
    return order


def summands(block, axis):
    count = lax.axis_size(axis)
    result = [block]
    for step in turns(count):
        result.append(lax.ppermute(block, axis, [(i, (i + step) % count) for i in range(count)]))
    return result


def turned(blocks, axis, group):
    count = lax.axis_size(axis)
    result = []
    for step, block in zip(turns(group), blocks):
        route = []
        for i in range(count):
            chip = i >> 1
            target = chip - chip % group + (chip + step) % group
            route.append((i, target << 1 | i & 1))
        result.append(lax.ppermute(block, axis, route))
    return result


def call(kernel, out_shape, args, specs, scratch=(), flops=0, name=None, outs=VMEM):
    return pl.pallas_call(
        kernel,
        out_shape=out_shape,
        in_specs=specs,
        out_specs=jax.tree.map(lambda _: outs, out_shape),
        scratch_shapes=list(scratch),
        compiler_params=pltpu.CompilerParams(vmem_limit_bytes=16 << 20),
        cost_estimate=pl.CostEstimate(
            flops=flops,
            transcendentals=0,
            bytes_accessed=sum(a.size * a.dtype.itemsize for a in args),
        ),
        name=name,
    )(*args)


def split_heads(source, wide, heads, length, store):
    wide[...] = source[...].astype(F32)
    for head in range(heads):
        store(head, wide[pl.ds(head, length, stride=heads), :])


def level_rows(sizes, scale, position_ref, pick_ref, table_ref, tw_ref):
    heads, length, levels, block, bits = sizes
    groups = table_ref.shape[0]
    lane = lax.broadcasted_iota(jnp.int32, (groups, levels), 1)
    factor = jnp.full((groups, levels), scale, F32)
    for j in range(bits):
        flag = (position_ref[0] >> j & 1).astype(F32) * scale
        factor = jnp.where(lane == levels - bits + j, flag, factor)
    group = lax.broadcasted_iota(jnp.int32, (groups, length), 0)
    one_hot = (group == pick_ref[...]).astype(F32)
    for head in range(heads):
        table = table_ref[:, head, :] * factor
        tw_ref[head] = lax.dot_general(one_hot, table, TN, precision=exact_mode, preferred_element_type=F32)


def local_forward(sizes, scale, position_ref, q_ref, k_ref, v_ref, g_ref, gain_hbm, pick_ref, table_ref,
                  inner_ref, p_ref, w_ref, qd_ref, kd_ref, vd_ref, gg_ref, tw_ref, wide, raw, gain_ref, sems):
    heads, length, levels, block, bits = sizes
    base = block.bit_length() - 1
    copies = [pltpu.make_async_copy(gain_hbm, gain_ref, sems.at[4])]
    for n, source in enumerate((k_ref, v_ref, q_ref, g_ref)):
        copies.append(pltpu.make_async_copy(source, raw.at[n], sems.at[n]))
    for copy in copies:
        copy.start()
    level_rows(sizes, scale, position_ref, pick_ref, table_ref, tw_ref)
    for n, target in enumerate((kd_ref, vd_ref, qd_ref)):
        def store(head, value, target=target):
            target[head] = value.astype(BF16)
        copies[n + 1].wait()
        split_heads(raw.at[n], wide, heads, length, store)
    copies[4].wait()
    copies[0].wait()

    def store_gain(head, value):
        gg_ref[head] = value * gain_ref[head:head + 1, :]
    split_heads(raw.at[3], wide, heads, length, store_gain)
    row = lax.broadcasted_iota(jnp.int32, (block, block), 0)
    column = lax.broadcasted_iota(jnp.int32, (block, block), 1)
    differs = row ^ column
    below = column <= row
    for head in range(heads):
        for i in range(length // block):
            rows = slice(i * block, (i + 1) * block)
            reach = slice(0, (i + 1) * block)
            def weight(level):
                return tw_ref[head, rows, level:level + 1]
            diagonal = jnp.broadcast_to(weight(0), (block, block))
            for level in range(1, base + 1):
                diagonal = jnp.where(differs >= 1 << (level - 1), weight(level), diagonal)
            diagonal = jnp.where(below, diagonal, 0.0)
            w_ref[head * (length // block) + i] = diagonal
            scores = dot(qd_ref[head, rows, :], kd_ref[head, reach, :], NT)
            parts = []
            for j in range(i):
                parts.append(scores[:, j * block:(j + 1) * block] * weight(base + (i ^ j).bit_length()))
            parts.append(scores[:, rows] * diagonal)
            for j, part in enumerate(parts):
                p_ref[head, rows, j * block:(j + 1) * block] = part.astype(BF16)
            inner_ref[head, rows, :] = dot(p_ref[head, rows, reach], vd_ref[head, reach, :], NN)


def cross_heads(sizes, heads_at, held_at, inner_ref, qd_ref, gg_ref, tw_ref, attn_ref, sums_ref, add=None):
    _, length, levels, block, bits = sizes
    for i in range(length // block):
        rows = slice(i * block, (i + 1) * block)
        squares = 0.0
        products = 0.0
        for h, head in enumerate(heads_at):
            total = inner_ref[head, rows, :]
            query = qd_ref[head, rows, :]
            for j in range(bits):
                at = levels - bits + j
                total = total + tw_ref[head, rows, at:at + 1] * dot(query, held_at(j, h), NN)
            attn_ref[h, rows, :] = total
            squares = squares + total * total
            products = products + total * gg_ref[head, rows, :]
        both = (squares, products)
        for n in range(2):
            row = jnp.sum(both[n].T, axis=0, keepdims=True)
            if add is not None:
                row = row + add[n:n + 1, rows]
            sums_ref[n:n + 1, rows] = row


def cross_mine(sizes, *refs):
    heads, length, levels, block, bits = sizes
    position_ref, inner_ref, qd_ref, gg_ref, tw_ref, near_ref = refs[:6]
    mine = refs[6:6 + bits - 1]
    attn_ref, sums_ref, held_ref = refs[-3:]
    half = heads // 2
    start = (position_ref[0] & 1) * half
    for h in range(half):
        held_ref[0, h] = near_ref[start + h].astype(BF16)
        for j in range(1, bits):
            held_ref[j, h] = mine[j - 1][h].astype(BF16)
    cross_heads(sizes, [start + h for h in range(half)], lambda j, h: held_ref[j, h],
                inner_ref, qd_ref, gg_ref, tw_ref, attn_ref, sums_ref)


def cross_other(sizes, *refs):
    heads, length, levels, block, bits = sizes
    position_ref, inner_ref, qd_ref, gg_ref, tw_ref, near_ref, add_ref = refs[:7]
    other = refs[7:7 + bits - 1]
    attn_ref, sums_ref, held_ref = refs[-3:]
    half = heads // 2
    start = (1 - (position_ref[0] & 1)) * half
    for h in range(half):
        held_ref[0, h] = near_ref[start + h].astype(BF16)
        for j in range(1, bits):
            held_ref[j, h] = other[j - 1][h].astype(BF16)
    cross_heads(sizes, [start + h for h in range(half)], lambda j, h: held_ref[j, h],
                inner_ref, qd_ref, gg_ref, tw_ref, attn_ref, sums_ref, add_ref)


def sibling(source, target, place):
    return ((source >> place) == (target >> place ^ 1)).astype(F32)


def combine_kernel(group, position_ref, *refs):
    far = group.bit_length() - 1
    received, targets = refs[:group - 1], refs[group - 1:]
    chip = (position_ref[0] >> 1) & (group - 1)
    for place in range(far):
        total = 0.0
        for step, block in zip(turns(group), received):
            source = (chip + group - step) & (group - 1)
            total = total + sibling(source, chip, place) * block[...]
        targets[place][...] = total


def message_kernel(group, position_ref, above_ref, keep_ref, came_ref, *targets):
    far = group.bit_length() - 1
    chip = (position_ref[0] >> 1) & (group - 1)
    for step, message in zip(turns(group), targets):
        target = (chip + step) & (group - 1)
        total = above_ref[...]
        for place in range(far):
            total = total + sibling(chip, target, place) * (keep_ref[place] + came_ref[place])
        message[...] = total


def spread(row, width):
    return jnp.broadcast_to(row, (width, row.shape[1])).T


def token_scales(features, sums):
    total = sums[0][...]
    for part in sums[1:]:
        total = total + part[...]
    inverse = lax.rsqrt(total[0:1] / features + epsilon)
    return inverse, inverse * inverse * inverse * (total[1:2] / features)


def grad_heads(sizes, heads_at, left_at, right_at, attn_ref, gg_ref, qd_ref, tw_ref, put_grad, scaled_ref, put_state):
    _, length, levels, block, bits = sizes
    width = attn_ref.shape[-1]
    for h, head in enumerate(heads_at):
        for i in range(length // block):
            rows = slice(i * block, (i + 1) * block)
            grad = (left_at(rows) * gg_ref[head, rows, :] - attn_ref[h, rows, :] * right_at(rows)).astype(BF16)
            put_grad(h, rows, grad)
            wide = grad.astype(F32)
            for j in range(bits):
                at = levels - bits + j
                scaled_ref[rows, j * width:(j + 1) * width] = (tw_ref[head, rows, at:at + 1] * wide).astype(BF16)
        product = dot(qd_ref[head], scaled_ref[...], TN)
        for j in range(bits):
            put_state(j, h, product[:, j * width:(j + 1) * width])


def grad_other(sizes, features, *refs):
    heads, length, levels, block, bits = sizes
    position_ref, attn_ref, gg_ref, qd_ref, tw_ref = refs[:5]
    sums = refs[5:-7]
    ag_ref, inverse_ref, left_ref, right_ref, first_ref, send_ref, scaled_ref = refs[-7:]
    half = heads // 2
    start = (1 - (position_ref[0] & 1)) * half
    width = attn_ref.shape[-1]
    inverse, beta = token_scales(features, sums)
    inverse_ref[...] = inverse
    for i in range(length // block):
        rows = slice(i * block, (i + 1) * block)
        left_ref[rows, :] = spread(inverse[:, rows], width)
        right_ref[rows, :] = spread(beta[:, rows], width)

    def put_grad(h, rows, grad):
        ag_ref[h, rows, :] = grad

    def put_state(j, h, value):
        if j == 0:
            first_ref[h] = value
        else:
            send_ref[j - 1, h] = value
    grad_heads(sizes, [start + h for h in range(half)], lambda rows: left_ref[rows, :], lambda rows: right_ref[rows, :],
               attn_ref, gg_ref, qd_ref, tw_ref, put_grad, scaled_ref, put_state)


def grad_mine(sizes, position_ref, attn_ref, far_ref, gg_ref, qd_ref, tw_ref, other_ref, left_ref, right_ref,
              held_mine_ref, held_other_ref, ag_ref, first_ref, keep_ref, attn_full_ref, held_ref, scaled_ref):
    heads, length, levels, block, bits = sizes
    half = heads // 2
    core = position_ref[0] & 1
    start = core * half
    away = (1 - core) * half

    def put_grad(h, rows, grad):
        ag_ref[start + h, rows, :] = grad

    def put_state(j, h, value):
        if j == 0:
            first_ref[h] = value
        else:
            keep_ref[j - 1, h] = value
    grad_heads(sizes, [start + h for h in range(half)], lambda rows: left_ref[rows, :], lambda rows: right_ref[rows, :],
               attn_ref, gg_ref, qd_ref, tw_ref, put_grad, scaled_ref, put_state)
    for h in range(half):
        ag_ref[away + h] = other_ref[h]
        attn_full_ref[start + h] = attn_ref[h]
        attn_full_ref[away + h] = far_ref[h]
        for j in range(bits):
            held_ref[j, start + h] = held_mine_ref[j, h]
            held_ref[j, away + h] = held_other_ref[j, h]


def local_backward(sizes, ag_ref, qd_ref, kd_ref, vd_ref, p_ref, w_ref, tw_ref, held_ref, attn_ref,
                   inverse_ref, gain_ref, normed_ref, dq_ref, dk_ref, dv_ref, weighted_ref):
    heads, length, levels, block, bits = sizes
    base = block.bit_length() - 1
    width = ag_ref.shape[-1]
    blocks = length // block
    for i in range(blocks):
        rows = slice(i * block, (i + 1) * block)
        reach = slice(0, (i + 1) * block)
        left = spread(inverse_ref[:, rows], width)
        for head in range(heads):
            put = pl.ds(i * block * heads + head, block, stride=heads)
            normed_ref[put, :] = attn_ref[head, rows, :] * left * gain_ref[head:head + 1, :]
            def weight(level):
                return tw_ref[head, rows, level:level + 1]
            grad = ag_ref[head, rows, :]
            scores = dot(grad, vd_ref[head, reach, :], NT)
            for j in range(i + 1):
                part = scores[:, j * block:(j + 1) * block]
                if j == i:
                    part = part * w_ref[head * blocks + i]
                else:
                    part = part * weight(base + (i ^ j).bit_length())
                weighted_ref[head, rows, j * block:(j + 1) * block] = part.astype(BF16)
            total = dot(weighted_ref[head, rows, reach], kd_ref[head, reach, :], NN)
            for j in range(bits):
                total = total + weight(levels - bits + j) * dot(grad, held_ref[j, head], NT)
            dq_ref[put, :] = total
    for head in range(heads):
        for j in range(blocks):
            cols = slice(j * block, (j + 1) * block)
            rest = slice(j * block, length)
            dk_ref[head, cols, :] = dot(weighted_ref[head, rest, cols], qd_ref[head, rest, :], TN)
            dv_ref[head, cols, :] = dot(p_ref[head, rest, cols], ag_ref[head, rest, :], TN)


def final_mine(sizes, position_ref, near_ref, total_ref, kd_ref, vd_ref, dk_ref, dv_ref, key_ref, value_ref):
    heads, length, block = sizes
    half = heads // 2
    core = position_ref[0] & 1
    keep = (1 - core).astype(F32)
    for h in range(half):
        head = core * half + h
        back = (total_ref[h] + keep * near_ref[h]).astype(BF16)
        key_ref[h] = dk_ref[head] + dot(vd_ref[head], back, NT)
        value_ref[h] = dv_ref[head] + dot(kd_ref[head], back, NN)


def final_other(sizes, position_ref, near_ref, total_ref, kd_ref, vd_ref, dk_ref, dv_ref, mine_key_ref, mine_value_ref,
                key_hbm, value_hbm, back_ref, key_ref, value_ref, sems):
    heads, length, block = sizes
    half = heads // 2
    core = position_ref[0] & 1
    keep = (1 - core).astype(F32)
    away = (1 - core) * half
    for h in range(half):
        back_ref[h] = (total_ref[h] + keep * near_ref[h]).astype(BF16)
    copies = []
    for i in range(length // block):
        rows = slice(i * block, (i + 1) * block)
        new = []
        for h in range(half):
            head = away + h
            back = back_ref[h]
            new.append((dk_ref[head, rows, :] + dot(vd_ref[head, rows, :], back, NT),
                        dv_ref[head, rows, :] + dot(kd_ref[head, rows, :], back, NN)))
        for h in range(half):
            old = (mine_key_ref[h, rows, :], mine_value_ref[h, rows, :])
            for n, target in enumerate((key_ref, value_ref)):
                low = jnp.where(core == 0, old[n], new[h][n])
                high = jnp.where(core == 0, new[h][n], old[n])
                target[pl.ds(i * block * heads + h, block, stride=heads), :] = low
                target[pl.ds(i * block * heads + half + h, block, stride=heads), :] = high
        chunk = pl.ds(i * block * heads, block * heads)
        for n, (source, target) in enumerate(((key_ref, key_hbm), (value_ref, value_hbm))):
            copy = pltpu.make_async_copy(source.at[chunk], target.at[chunk], sems.at[n, i])
            copy.start()
            copies.append(copy)
    for copy in copies:
        copy.wait()


def shards(query_rows, key_rows, value_rows, level_pick, level_table, norm_gain, out_grad):
    length, heads, width = query_rows.shape
    groups, _, levels = level_table.shape
    local_bits = length.bit_length() - 1
    bits = lax.axis_size("seq").bit_length() - 1
    block = min(128, length)
    half = heads // 2
    scale = width ** (-0.5)
    position = lax.axis_index("seq").astype(jnp.int32)
    place_arg = position.reshape(1)
    shape = jax.ShapeDtypeStruct

    own = jnp.einsum("shd,she->hde", key_rows, value_rows, preferred_element_type=F32)
    near = swapped(own, "seq", 0)
    pair = own + near

    block_sum = lax.dynamic_slice(
        pair, ((position & 1) * half, 0, 0), (half, width, width), allow_negative_indices=False
    )
    far = min(bits - 1, 2)
    group = 1 << far
    received = turned([block_sum] * (group - 1), "seq", group)

    rows = length * heads
    flat = lambda a: a.reshape(rows, width)
    local_flops = heads * length * length * width
    sizes = (heads, length, levels, block, bits)
    inner, probs, diag, qd, kd, vd, gg, weights = call(
        functools.partial(local_forward, sizes, scale),
        (
            shape((heads, length, width), F32),
            shape((heads, length, length), BF16),
            shape((heads * (length // block), block, block), F32),
            shape((heads, length, width), BF16),
            shape((heads, length, width), BF16),
            shape((heads, length, width), BF16),
            shape((heads, length, width), F32),
            shape((heads, length, levels), F32),
        ),
        (
            place_arg,
            flat(query_rows),
            flat(key_rows),
            flat(value_rows),
            flat(out_grad),
            norm_gain,
            level_pick.reshape(1, length),
            level_table,
        ),
        [SMEM, HBM, HBM, HBM, HBM, HBM, VMEM, VMEM],
        [
            pltpu.VMEM((rows, width), F32),
            pltpu.VMEM((4, rows, width), BF16),
            pltpu.VMEM((heads, width), F32),
            pltpu.SemaphoreType.DMA((5,)),
        ],
        flops=4 * local_flops,
        name="local_forward",
    )
    inner, received = lax.optimization_barrier((inner, received))
    state = shape((half, width, width), F32)
    mine = call(
        functools.partial(combine_kernel, group),
        (state,) * far,
        (place_arg, *received),
        [SMEM] + [VMEM] * (group - 1),
        name="far_states",
    )
    mine = list(mine)
    block_sum = functools.reduce(jnp.add, received, block_sum)
    for place in range(far + 1, bits):
        mine.append(swapped(block_sum, "seq", place))
        block_sum = block_sum + mine[-1]
    others = [swapped(partner, "seq", 0) for partner in mine]
    cross_flops = bits * heads * length * width * width
    cross_shapes = (
        shape((half, length, width), F32),
        shape((2, length), F32),
        shape((bits, half, width, width), BF16),
    )
    attn_mine, sums, held_mine = call(
        functools.partial(cross_mine, sizes),
        cross_shapes,
        (place_arg, inner, qd, gg, weights, near, *mine),
        [SMEM] + [VMEM] * (5 + len(mine)),
        flops=cross_flops,
        name="cross_mine",
    )
    attn_other, sums, held_other = call(
        functools.partial(cross_other, sizes),
        cross_shapes,
        (place_arg, inner, qd, gg, weights, near, sums, *others),
        [SMEM] + [VMEM] * (6 + len(others)),
        flops=cross_flops,
        name="cross_other",
    )
    features = heads * width * lax.axis_size("heads")
    parts = summands(sums, "heads")
    grad_far, inverse, left, right, first_other, send = call(
        functools.partial(grad_other, sizes, features),
        (
            shape((half, length, width), BF16),
            shape((1, length), F32),
            shape((length, width), F32),
            shape((length, width), F32),
            shape((half, width, width), F32),
            shape((bits - 1, half, width, width), F32),
        ),
        (place_arg, attn_other, gg, qd, weights, *parts),
        [SMEM] + [VMEM] * (4 + len(parts)),
        [pltpu.VMEM((length, bits * width), BF16)],
        flops=cross_flops,
        name="state_grads_other",
    )
    attn_grad, first_mine, keep, attn, held = call(
        functools.partial(grad_mine, sizes),
        (
            shape((heads, length, width), BF16),
            shape((half, width, width), F32),
            shape((bits - 1, half, width, width), F32),
            shape((heads, length, width), F32),
            shape((bits, heads, width, width), BF16),
        ),
        (place_arg, attn_mine, attn_other, gg, qd, weights, grad_far, left, right, held_mine, held_other),
        [SMEM] + [VMEM] * 10,
        [pltpu.VMEM((length, bits * width), BF16)],
        flops=cross_flops,
        name="state_grads_mine",
    )
    came = swapped(send, "seq", 0)
    above = jnp.zeros((half, width, width), F32)
    for place in reversed(range(far + 1, bits)):
        above = above + swapped(above + keep[place - 1] + came[place - 1], "seq", place)
    messages = call(
        functools.partial(message_kernel, group),
        (state,) * (group - 1),
        (place_arg, above, keep, came),
        [SMEM] + [VMEM] * 3,
        name="far_messages",
    )
    landed = turned(messages, "seq", group)
    near_other = swapped(first_mine, "seq", 0)
    near_mine = swapped(first_other, "seq", 0)

    normed, query_grad, key_part, value_part = call(
        functools.partial(local_backward, sizes),
        (
            shape((rows, width), F32),
            shape((rows, width), F32),
            shape((heads, length, width), F32),
            shape((heads, length, width), F32),
        ),
        (attn_grad, qd, kd, vd, probs, diag, weights, held, attn, inverse, norm_gain),
        [VMEM] * 11,
        [pltpu.VMEM((heads, length, length), BF16)],
        flops=8 * local_flops,
        name="local_backward",
    )
    landed, key_part = lax.optimization_barrier((landed, key_part))
    total = functools.reduce(jnp.add, landed, above)
    other = swapped(total, "seq", 0)

    final_sizes = (heads, length, block)
    final_flops = 2 * heads * length * width * width
    key_mine, value_mine = call(
        functools.partial(final_mine, final_sizes),
        (shape((half, length, width), F32), shape((half, length, width), F32)),
        (place_arg, near_mine, total, kd, vd, key_part, value_part),
        [SMEM] + [VMEM] * 6,
        flops=final_flops,
        name="key_value_mine",
    )
    key_grad, value_grad = call(
        functools.partial(final_other, final_sizes),
        (shape((rows, width), F32), shape((rows, width), F32)),
        (place_arg, near_other, other, kd, vd, key_part, value_part, key_mine, value_mine),
        [SMEM] + [VMEM] * 8,
        [
            pltpu.VMEM((half, width, width), BF16),
            pltpu.VMEM((rows, width), F32),
            pltpu.VMEM((rows, width), F32),
            pltpu.SemaphoreType.DMA((2, length // block)),
        ],
        flops=final_flops,
        name="key_value_other",
        outs=HBM,
    )
    return tuple(a.reshape(length, heads, width) for a in (normed, query_grad, key_grad, value_grad))


def solution(mesh):
    in_specs = (
        P("seq", "heads", None),
        P("seq", "heads", None),
        P("seq", "heads", None),
        P("seq"),
        P(None, "heads", None),
        P("heads", None),
        P("seq", "heads", None),
    )
    out_specs = (
        P("seq", "heads", None),
        P("seq", "heads", None),
        P("seq", "heads", None),
        P("seq", "heads", None),
    )
    return jax.shard_map(shards, mesh=mesh, in_specs=in_specs, out_specs=out_specs, check_vma=False)
```

```python
import functools

import jax
import jax.numpy as jnp
from jax import lax
from jax.experimental import pallas as pl
from jax.experimental.pallas import tpu as pltpu
from jax.sharding import PartitionSpec as P

exact_mode = lax.Precision.HIGHEST
epsilon = 1e-06
F32 = jnp.float32
BF16 = jnp.bfloat16
VMEM = pl.BlockSpec(memory_space=pltpu.VMEM)
HBM = pl.BlockSpec(memory_space=pltpu.HBM)
SMEM = pl.BlockSpec(memory_space=pltpu.SMEM)
NT = (((1,), (1,)), ((), ()))
TN = (((0,), (0,)), ((), ()))
NN = (((1,), (0,)), ((), ()))


def dot(left, right, dims):
    return lax.dot_general(left, right, dims, preferred_element_type=F32)


def swapped(block, axis, distance):
    count = lax.axis_size(axis)
    route = []
    for low in range(count):
        high = low | 1 << distance
        if high != low and high < count:
            route += [(low, high), (high, low)]
    return lax.ppermute(block, axis, route)


def turns(count):
    order = []
    for step in range(1, count // 2 + 1):
        order += [step] if 2 * step == count else [step, count - step]
    return order


def swaps(group):
    return list(range(group - 1, 0, -1))


def summands(block, axis):
    count = lax.axis_size(axis)
    result = [block]
    for step in turns(count):
        result.append(lax.ppermute(block, axis, [(i, (i + step) % count) for i in range(count)]))
    return result


def turned(blocks, axis, group):
    count = lax.axis_size(axis)
    result = []
    for step, block in zip(swaps(group), blocks):
        route = []
        for i in range(count):
            chip = i >> 1
            target = chip - chip % group + (chip % group ^ step)
            route.append((i, target << 1 | i & 1))
        result.append(lax.ppermute(block, axis, route))
    return result


def call(kernel, out_shape, args, specs, scratch=(), flops=0, name=None, outs=VMEM):
    return pl.pallas_call(
        kernel,
        out_shape=out_shape,
        in_specs=specs,
        out_specs=jax.tree.map(lambda _: outs, out_shape),
        scratch_shapes=list(scratch),
        compiler_params=pltpu.CompilerParams(vmem_limit_bytes=16 << 20),
        cost_estimate=pl.CostEstimate(
            flops=flops,
            transcendentals=0,
            bytes_accessed=sum(a.size * a.dtype.itemsize for a in args),
        ),
        name=name,
    )(*args)


def split_heads(source, wide, heads, length, store):
    wide[...] = source[...].astype(F32)
    for head in range(heads):
        store(head, wide[pl.ds(head, length, stride=heads), :])


def level_rows(sizes, scale, position_ref, pick_ref, table_ref, tw_ref):
    heads, length, levels, block, bits = sizes
    groups = table_ref.shape[0]
    lane = lax.broadcasted_iota(jnp.int32, (groups, levels), 1)
    factor = jnp.full((groups, levels), scale, F32)
    for j in range(bits):
        flag = (position_ref[0] >> j & 1).astype(F32) * scale
        factor = jnp.where(lane == levels - bits + j, flag, factor)
    group = lax.broadcasted_iota(jnp.int32, (groups, length), 0)
    one_hot = (group == pick_ref[...]).astype(F32)
    for head in range(heads):
        table = table_ref[:, head, :] * factor
        tw_ref[head] = lax.dot_general(one_hot, table, TN, precision=exact_mode, preferred_element_type=F32)


def local_forward(sizes, scale, position_ref, q_ref, k_ref, v_ref, g_ref, gain_hbm, pick_ref, table_ref,
                  inner_ref, p_ref, w_ref, qd_ref, kd_ref, vd_ref, gg_ref, tw_ref, wide, raw, gain_ref, sems):
    heads, length, levels, block, bits = sizes
    base = block.bit_length() - 1
    copies = [pltpu.make_async_copy(gain_hbm, gain_ref, sems.at[4])]
    for n, source in enumerate((k_ref, v_ref, q_ref, g_ref)):
        copies.append(pltpu.make_async_copy(source, raw.at[n], sems.at[n]))
    for copy in copies:
        copy.start()
    level_rows(sizes, scale, position_ref, pick_ref, table_ref, tw_ref)
    for n, target in enumerate((kd_ref, vd_ref, qd_ref)):
        def store(head, value, target=target):
            target[head] = value.astype(BF16)
        copies[n + 1].wait()
        split_heads(raw.at[n], wide, heads, length, store)
    copies[4].wait()
    copies[0].wait()

    def store_gain(head, value):
        gg_ref[head] = value * gain_ref[head:head + 1, :]
    split_heads(raw.at[3], wide, heads, length, store_gain)
    row = lax.broadcasted_iota(jnp.int32, (block, block), 0)
    column = lax.broadcasted_iota(jnp.int32, (block, block), 1)
    differs = row ^ column
    below = column <= row
    for head in range(heads):
        for i in range(length // block):
            rows = slice(i * block, (i + 1) * block)
            reach = slice(0, (i + 1) * block)
            def weight(level):
                return tw_ref[head, rows, level:level + 1]
            diagonal = jnp.broadcast_to(weight(0), (block, block))
            for level in range(1, base + 1):
                diagonal = jnp.where(differs >= 1 << (level - 1), weight(level), diagonal)
            diagonal = jnp.where(below, diagonal, 0.0)
            w_ref[head * (length // block) + i] = diagonal
            scores = dot(qd_ref[head, rows, :], kd_ref[head, reach, :], NT)
            parts = []
            for j in range(i):
                parts.append(scores[:, j * block:(j + 1) * block] * weight(base + (i ^ j).bit_length()))
            parts.append(scores[:, rows] * diagonal)
            for j, part in enumerate(parts):
                p_ref[head, rows, j * block:(j + 1) * block] = part.astype(BF16)
            inner_ref[head, rows, :] = dot(p_ref[head, rows, reach], vd_ref[head, reach, :], NN)


def cross_heads(sizes, heads_at, held_at, inner_ref, qd_ref, gg_ref, tw_ref, attn_ref, sums_ref, add=None):
    _, length, levels, block, bits = sizes
    for i in range(length // block):
        rows = slice(i * block, (i + 1) * block)
        squares = 0.0
        products = 0.0
        for h, head in enumerate(heads_at):
            total = inner_ref[head, rows, :]
            query = qd_ref[head, rows, :]
            for j in range(bits):
                at = levels - bits + j
                total = total + tw_ref[head, rows, at:at + 1] * dot(query, held_at(j, h), NN)
            attn_ref[h, rows, :] = total
            squares = squares + total * total
            products = products + total * gg_ref[head, rows, :]
        both = (squares, products)
        for n in range(2):
            row = jnp.sum(both[n].T, axis=0, keepdims=True)
            if add is not None:
                row = row + add[n:n + 1, rows]
            sums_ref[n:n + 1, rows] = row


def cross_mine(sizes, *refs):
    heads, length, levels, block, bits = sizes
    position_ref, inner_ref, qd_ref, gg_ref, tw_ref, near_ref = refs[:6]
    mine = refs[6:6 + bits - 1]
    attn_ref, sums_ref, held_ref = refs[-3:]
    half = heads // 2
    start = (position_ref[0] & 1) * half
    for h in range(half):
        held_ref[0, h] = near_ref[start + h].astype(BF16)
        for j in range(1, bits):
            held_ref[j, h] = mine[j - 1][h].astype(BF16)
    cross_heads(sizes, [start + h for h in range(half)], lambda j, h: held_ref[j, h],
                inner_ref, qd_ref, gg_ref, tw_ref, attn_ref, sums_ref)


def cross_other(sizes, *refs):
    heads, length, levels, block, bits = sizes
    position_ref, inner_ref, qd_ref, gg_ref, tw_ref, near_ref, add_ref = refs[:7]
    other = refs[7:7 + bits - 1]
    attn_ref, sums_ref, held_ref = refs[-3:]
    half = heads // 2
    start = (1 - (position_ref[0] & 1)) * half
    for h in range(half):
        held_ref[0, h] = near_ref[start + h].astype(BF16)
        for j in range(1, bits):
            held_ref[j, h] = other[j - 1][h].astype(BF16)
    cross_heads(sizes, [start + h for h in range(half)], lambda j, h: held_ref[j, h],
                inner_ref, qd_ref, gg_ref, tw_ref, attn_ref, sums_ref, add_ref)


def sibling(source, target, place):
    return ((source >> place) == (target >> place ^ 1)).astype(F32)


def combine_kernel(group, position_ref, *refs):
    far = group.bit_length() - 1
    received, targets = refs[:group - 1], refs[group - 1:]
    chip = (position_ref[0] >> 1) & (group - 1)
    for place in range(far):
        total = 0.0
        for step, block in zip(swaps(group), received):
            source = chip ^ step
            total = total + sibling(source, chip, place) * block[...]
        targets[place][...] = total


def message_kernel(group, position_ref, above_ref, keep_ref, came_ref, *targets):
    far = group.bit_length() - 1
    chip = (position_ref[0] >> 1) & (group - 1)
    for step, message in zip(swaps(group), targets):
        target = chip ^ step
        total = above_ref[...]
        for place in range(far):
            total = total + sibling(chip, target, place) * (keep_ref[place] + came_ref[place])
        message[...] = total


def spread(row, width):
    return jnp.broadcast_to(row, (width, row.shape[1])).T


def token_scales(features, sums):
    total = sums[0][...]
    for part in sums[1:]:
        total = total + part[...]
    inverse = lax.rsqrt(total[0:1] / features + epsilon)
    return inverse, inverse * inverse * inverse * (total[1:2] / features)


def grad_heads(sizes, heads_at, left_at, right_at, attn_ref, gg_ref, qd_ref, tw_ref, put_grad, scaled_ref, put_state):
    _, length, levels, block, bits = sizes
    width = attn_ref.shape[-1]
    for h, head in enumerate(heads_at):
        for i in range(length // block):
            rows = slice(i * block, (i + 1) * block)
            grad = (left_at(rows) * gg_ref[head, rows, :] - attn_ref[h, rows, :] * right_at(rows)).astype(BF16)
            put_grad(h, rows, grad)
            wide = grad.astype(F32)
            for j in range(bits):
                at = levels - bits + j
                scaled_ref[rows, j * width:(j + 1) * width] = (tw_ref[head, rows, at:at + 1] * wide).astype(BF16)
        product = dot(qd_ref[head], scaled_ref[...], TN)
        for j in range(bits):
            put_state(j, h, product[:, j * width:(j + 1) * width])


def grad_other(sizes, features, *refs):
    heads, length, levels, block, bits = sizes
    position_ref, attn_ref, gg_ref, qd_ref, tw_ref = refs[:5]
    sums = refs[5:-7]
    ag_ref, inverse_ref, left_ref, right_ref, first_ref, send_ref, scaled_ref = refs[-7:]
    half = heads // 2
    start = (1 - (position_ref[0] & 1)) * half
    width = attn_ref.shape[-1]
    inverse, beta = token_scales(features, sums)
    inverse_ref[...] = inverse
    for i in range(length // block):
        rows = slice(i * block, (i + 1) * block)
        left_ref[rows, :] = spread(inverse[:, rows], width)
        right_ref[rows, :] = spread(beta[:, rows], width)

    def put_grad(h, rows, grad):
        ag_ref[h, rows, :] = grad

    def put_state(j, h, value):
        if j == 0:
            first_ref[h] = value
        else:
            send_ref[j - 1, h] = value
    grad_heads(sizes, [start + h for h in range(half)], lambda rows: left_ref[rows, :], lambda rows: right_ref[rows, :],
               attn_ref, gg_ref, qd_ref, tw_ref, put_grad, scaled_ref, put_state)


def grad_mine(sizes, position_ref, attn_ref, far_ref, gg_ref, qd_ref, tw_ref, other_ref, left_ref, right_ref,
              held_mine_ref, held_other_ref, ag_ref, first_ref, keep_ref, attn_full_ref, held_ref, scaled_ref):
    heads, length, levels, block, bits = sizes
    half = heads // 2
    core = position_ref[0] & 1
    start = core * half
    away = (1 - core) * half

    def put_grad(h, rows, grad):
        ag_ref[start + h, rows, :] = grad

    def put_state(j, h, value):
        if j == 0:
            first_ref[h] = value
        else:
            keep_ref[j - 1, h] = value
    grad_heads(sizes, [start + h for h in range(half)], lambda rows: left_ref[rows, :], lambda rows: right_ref[rows, :],
               attn_ref, gg_ref, qd_ref, tw_ref, put_grad, scaled_ref, put_state)
    for h in range(half):
        ag_ref[away + h] = other_ref[h]
        attn_full_ref[start + h] = attn_ref[h]
        attn_full_ref[away + h] = far_ref[h]
        for j in range(bits):
            held_ref[j, start + h] = held_mine_ref[j, h]
            held_ref[j, away + h] = held_other_ref[j, h]


def local_backward(sizes, ag_ref, qd_ref, kd_ref, vd_ref, p_ref, w_ref, tw_ref, held_ref, attn_ref,
                   inverse_ref, gain_ref, normed_ref, dq_ref, dk_ref, dv_ref, weighted_ref):
    heads, length, levels, block, bits = sizes
    base = block.bit_length() - 1
    width = ag_ref.shape[-1]
    blocks = length // block
    for i in range(blocks):
        rows = slice(i * block, (i + 1) * block)
        reach = slice(0, (i + 1) * block)
        left = spread(inverse_ref[:, rows], width)
        for head in range(heads):
            put = pl.ds(i * block * heads + head, block, stride=heads)
            normed_ref[put, :] = attn_ref[head, rows, :] * left * gain_ref[head:head + 1, :]
            def weight(level):
                return tw_ref[head, rows, level:level + 1]
            grad = ag_ref[head, rows, :]
            scores = dot(grad, vd_ref[head, reach, :], NT)
            for j in range(i + 1):
                part = scores[:, j * block:(j + 1) * block]
                if j == i:
                    part = part * w_ref[head * blocks + i]
                else:
                    part = part * weight(base + (i ^ j).bit_length())
                weighted_ref[head, rows, j * block:(j + 1) * block] = part.astype(BF16)
            total = dot(weighted_ref[head, rows, reach], kd_ref[head, reach, :], NN)
            for j in range(bits):
                total = total + weight(levels - bits + j) * dot(grad, held_ref[j, head], NT)
            dq_ref[put, :] = total
    for head in range(heads):
        for j in range(blocks):
            cols = slice(j * block, (j + 1) * block)
            rest = slice(j * block, length)
            dk_ref[head, cols, :] = dot(weighted_ref[head, rest, cols], qd_ref[head, rest, :], TN)
            dv_ref[head, cols, :] = dot(p_ref[head, rest, cols], ag_ref[head, rest, :], TN)


def final_mine(sizes, position_ref, near_ref, total_ref, kd_ref, vd_ref, dk_ref, dv_ref, key_ref, value_ref):
    heads, length, block = sizes
    half = heads // 2
    core = position_ref[0] & 1
    keep = (1 - core).astype(F32)
    for h in range(half):
        head = core * half + h
        back = (total_ref[h] + keep * near_ref[h]).astype(BF16)
        key_ref[h] = dk_ref[head] + dot(vd_ref[head], back, NT)
        value_ref[h] = dv_ref[head] + dot(kd_ref[head], back, NN)


def final_other(sizes, position_ref, near_ref, total_ref, kd_ref, vd_ref, dk_ref, dv_ref, mine_key_ref, mine_value_ref,
                key_hbm, value_hbm, back_ref, key_ref, value_ref, sems):
    heads, length, block = sizes
    half = heads // 2
    core = position_ref[0] & 1
    keep = (1 - core).astype(F32)
    away = (1 - core) * half
    for h in range(half):
        back_ref[h] = (total_ref[h] + keep * near_ref[h]).astype(BF16)
    copies = []
    for i in range(length // block):
        rows = slice(i * block, (i + 1) * block)
        new = []
        for h in range(half):
            head = away + h
            back = back_ref[h]
            new.append((dk_ref[head, rows, :] + dot(vd_ref[head, rows, :], back, NT),
                        dv_ref[head, rows, :] + dot(kd_ref[head, rows, :], back, NN)))
        for h in range(half):
            old = (mine_key_ref[h, rows, :], mine_value_ref[h, rows, :])
            for n, target in enumerate((key_ref, value_ref)):
                low = jnp.where(core == 0, old[n], new[h][n])
                high = jnp.where(core == 0, new[h][n], old[n])
                target[pl.ds(i * block * heads + h, block, stride=heads), :] = low
                target[pl.ds(i * block * heads + half + h, block, stride=heads), :] = high
        chunk = pl.ds(i * block * heads, block * heads)
        for n, (source, target) in enumerate(((key_ref, key_hbm), (value_ref, value_hbm))):
            copy = pltpu.make_async_copy(source.at[chunk], target.at[chunk], sems.at[n, i])
            copy.start()
            copies.append(copy)
    for copy in copies:
        copy.wait()


def shards(query_rows, key_rows, value_rows, level_pick, level_table, norm_gain, out_grad):
    length, heads, width = query_rows.shape
    groups, _, levels = level_table.shape
    local_bits = length.bit_length() - 1
    bits = lax.axis_size("seq").bit_length() - 1
    block = min(128, length)
    half = heads // 2
    scale = width ** (-0.5)
    position = lax.axis_index("seq").astype(jnp.int32)
    place_arg = position.reshape(1)
    shape = jax.ShapeDtypeStruct

    own = jnp.einsum("shd,she->hde", key_rows, value_rows, preferred_element_type=F32)
    near = swapped(own, "seq", 0)
    pair = own + near

    block_sum = lax.dynamic_slice(
        pair, ((position & 1) * half, 0, 0), (half, width, width), allow_negative_indices=False
    )
    far = min(bits - 1, 2)
    group = 1 << far
    received = turned([block_sum] * (group - 1), "seq", group)

    rows = length * heads
    flat = lambda a: a.reshape(rows, width)
    local_flops = heads * length * length * width
    sizes = (heads, length, levels, block, bits)
    inner, probs, diag, qd, kd, vd, gg, weights = call(
        functools.partial(local_forward, sizes, scale),
        (
            shape((heads, length, width), F32),
            shape((heads, length, length), BF16),
            shape((heads * (length // block), block, block), F32),
            shape((heads, length, width), BF16),
            shape((heads, length, width), BF16),
            shape((heads, length, width), BF16),
            shape((heads, length, width), F32),
            shape((heads, length, levels), F32),
        ),
        (
            place_arg,
            flat(query_rows),
            flat(key_rows),
            flat(value_rows),
            flat(out_grad),
            norm_gain,
            level_pick.reshape(1, length),
            level_table,
        ),
        [SMEM, HBM, HBM, HBM, HBM, HBM, VMEM, VMEM],
        [
            pltpu.VMEM((rows, width), F32),
            pltpu.VMEM((4, rows, width), BF16),
            pltpu.VMEM((heads, width), F32),
            pltpu.SemaphoreType.DMA((5,)),
        ],
        flops=4 * local_flops,
        name="local_forward",
    )
    inner, received = lax.optimization_barrier((inner, received))
    state = shape((half, width, width), F32)
    mine = call(
        functools.partial(combine_kernel, group),
        (state,) * far,
        (place_arg, *received),
        [SMEM] + [VMEM] * (group - 1),
        name="far_states",
    )
    mine = list(mine)
    block_sum = functools.reduce(jnp.add, received, block_sum)
    for place in range(far + 1, bits):
        mine.append(swapped(block_sum, "seq", place))
        block_sum = block_sum + mine[-1]
    others = [swapped(partner, "seq", 0) for partner in mine]
    cross_flops = bits * heads * length * width * width
    cross_shapes = (
        shape((half, length, width), F32),
        shape((2, length), F32),
        shape((bits, half, width, width), BF16),
    )
    attn_mine, sums, held_mine = call(
        functools.partial(cross_mine, sizes),
        cross_shapes,
        (place_arg, inner, qd, gg, weights, near, *mine),
        [SMEM] + [VMEM] * (5 + len(mine)),
        flops=cross_flops,
        name="cross_mine",
    )
    attn_other, sums, held_other = call(
        functools.partial(cross_other, sizes),
        cross_shapes,
        (place_arg, inner, qd, gg, weights, near, sums, *others),
        [SMEM] + [VMEM] * (6 + len(others)),
        flops=cross_flops,
        name="cross_other",
    )
    features = heads * width * lax.axis_size("heads")
    parts = summands(sums, "heads")
    grad_far, inverse, left, right, first_other, send = call(
        functools.partial(grad_other, sizes, features),
        (
            shape((half, length, width), BF16),
            shape((1, length), F32),
            shape((length, width), F32),
            shape((length, width), F32),
            shape((half, width, width), F32),
            shape((bits - 1, half, width, width), F32),
        ),
        (place_arg, attn_other, gg, qd, weights, *parts),
        [SMEM] + [VMEM] * (4 + len(parts)),
        [pltpu.VMEM((length, bits * width), BF16)],
        flops=cross_flops,
        name="state_grads_other",
    )
    attn_grad, first_mine, keep, attn, held = call(
        functools.partial(grad_mine, sizes),
        (
            shape((heads, length, width), BF16),
            shape((half, width, width), F32),
            shape((bits - 1, half, width, width), F32),
            shape((heads, length, width), F32),
            shape((bits, heads, width, width), BF16),
        ),
        (place_arg, attn_mine, attn_other, gg, qd, weights, grad_far, left, right, held_mine, held_other),
        [SMEM] + [VMEM] * 10,
        [pltpu.VMEM((length, bits * width), BF16)],
        flops=cross_flops,
        name="state_grads_mine",
    )
    came = swapped(send, "seq", 0)
    above = jnp.zeros((half, width, width), F32)
    for place in reversed(range(far + 1, bits)):
        above = above + swapped(above + keep[place - 1] + came[place - 1], "seq", place)
    messages = call(
        functools.partial(message_kernel, group),
        (state,) * (group - 1),
        (place_arg, above, keep, came),
        [SMEM] + [VMEM] * 3,
        name="far_messages",
    )
    landed = turned(messages, "seq", group)
    near_other = swapped(first_mine, "seq", 0)
    near_mine = swapped(first_other, "seq", 0)

    normed, query_grad, key_part, value_part = call(
        functools.partial(local_backward, sizes),
        (
            shape((rows, width), F32),
            shape((rows, width), F32),
            shape((heads, length, width), F32),
            shape((heads, length, width), F32),
        ),
        (attn_grad, qd, kd, vd, probs, diag, weights, held, attn, inverse, norm_gain),
        [VMEM] * 11,
        [pltpu.VMEM((heads, length, length), BF16)],
        flops=8 * local_flops,
        name="local_backward",
    )
    landed, key_part = lax.optimization_barrier((landed, key_part))
    total = functools.reduce(jnp.add, landed, above)
    other = swapped(total, "seq", 0)

    final_sizes = (heads, length, block)
    final_flops = 2 * heads * length * width * width
    key_mine, value_mine = call(
        functools.partial(final_mine, final_sizes),
        (shape((half, length, width), F32), shape((half, length, width), F32)),
        (place_arg, near_mine, total, kd, vd, key_part, value_part),
        [SMEM] + [VMEM] * 6,
        flops=final_flops,
        name="key_value_mine",
    )
    key_grad, value_grad = call(
        functools.partial(final_other, final_sizes),
        (shape((rows, width), F32), shape((rows, width), F32)),
        (place_arg, near_other, other, kd, vd, key_part, value_part, key_mine, value_mine),
        [SMEM] + [VMEM] * 8,
        [
            pltpu.VMEM((half, width, width), BF16),
            pltpu.VMEM((rows, width), F32),
            pltpu.VMEM((rows, width), F32),
            pltpu.SemaphoreType.DMA((2, length // block)),
        ],
        flops=final_flops,
        name="key_value_other",
        outs=HBM,
    )
    return tuple(a.reshape(length, heads, width) for a in (normed, query_grad, key_grad, value_grad))


def solution(mesh):
    in_specs = (
        P("seq", "heads", None),
        P("seq", "heads", None),
        P("seq", "heads", None),
        P("seq"),
        P(None, "heads", None),
        P("heads", None),
        P("seq", "heads", None),
    )
    out_specs = (
        P("seq", "heads", None),
        P("seq", "heads", None),
        P("seq", "heads", None),
        P("seq", "heads", None),
    )
    return jax.shard_map(shards, mesh=mesh, in_specs=in_specs, out_specs=out_specs, check_vma=False)
```

```python
import functools

import jax
import jax.numpy as jnp
from jax import lax
from jax.experimental import pallas as pl
from jax.experimental.pallas import tpu as pltpu
from jax.sharding import PartitionSpec as P

exact_mode = lax.Precision.HIGHEST
epsilon = 1e-06
F32 = jnp.float32
BF16 = jnp.bfloat16
VMEM = pl.BlockSpec(memory_space=pltpu.VMEM)
HBM = pl.BlockSpec(memory_space=pltpu.HBM)
SMEM = pl.BlockSpec(memory_space=pltpu.SMEM)
NT = (((1,), (1,)), ((), ()))
TN = (((0,), (0,)), ((), ()))
NN = (((1,), (0,)), ((), ()))


def dot(left, right, dims):
    return lax.dot_general(left, right, dims, preferred_element_type=F32)


def swapped(block, axis, distance):
    count = lax.axis_size(axis)
    route = []
    for low in range(count):
        high = low | 1 << distance
        if high != low and high < count:
            route += [(low, high), (high, low)]
    return lax.ppermute(block, axis, route)


def turns(count):
    order = []
    for step in range(1, count // 2 + 1):
        order += [step] if 2 * step == count else [step, count - step]
    return order


def swaps(group):
    return list(range(group - 1, 0, -1))


def summands(block, axis):
    count = lax.axis_size(axis)
    result = [block]
    for step in turns(count):
        result.append(lax.ppermute(block, axis, [(i, (i + step) % count) for i in range(count)]))
    return result


def turned(blocks, axis, group):
    count = lax.axis_size(axis)
    result = []
    for step, block in zip(swaps(group), blocks):
        route = []
        for i in range(count):
            chip = i >> 1
            target = chip - chip % group + (chip % group ^ step)
            route.append((i, target << 1 | i & 1))
        result.append(lax.ppermute(block, axis, route))
    return result


def call(kernel, out_shape, args, specs, scratch=(), flops=0, name=None, outs=VMEM, aliases={}):
    return pl.pallas_call(
        kernel,
        out_shape=out_shape,
        in_specs=specs,
        out_specs=jax.tree.map(lambda _: outs, out_shape),
        scratch_shapes=list(scratch),
        compiler_params=pltpu.CompilerParams(vmem_limit_bytes=16 << 20),
        cost_estimate=pl.CostEstimate(
            flops=flops,
            transcendentals=0,
            bytes_accessed=sum(a.size * a.dtype.itemsize for a in args),
        ),
        name=name,
        input_output_aliases=aliases,
    )(*args)


def split_heads(source, wide, heads, length, store):
    wide[...] = source[...].astype(F32)
    for head in range(heads):
        store(head, wide[pl.ds(head, length, stride=heads), :])


def level_rows(sizes, scale, position_ref, pick_ref, table_ref, tw_ref):
    heads, length, levels, block, bits = sizes
    groups = table_ref.shape[0]
    lane = lax.broadcasted_iota(jnp.int32, (groups, levels), 1)
    factor = jnp.full((groups, levels), scale, F32)
    for j in range(bits):
        flag = (position_ref[0] >> j & 1).astype(F32) * scale
        factor = jnp.where(lane == levels - bits + j, flag, factor)
    group = lax.broadcasted_iota(jnp.int32, (groups, length), 0)
    one_hot = (group == pick_ref[...]).astype(F32)
    for head in range(heads):
        table = table_ref[:, head, :] * factor
        tw_ref[head] = lax.dot_general(one_hot, table, TN, precision=exact_mode, preferred_element_type=F32)


def gain_rows(sizes, g_ref, gain_ref, gg_ref, wide):
    heads, length = sizes

    def store(head, value):
        gg_ref[head] = value * gain_ref[head:head + 1, :]
    split_heads(g_ref, wide, heads, length, store)


def local_forward(sizes, q_ref, k_ref, v_ref, tw_ref, inner_ref, p_ref, w_ref, qd_ref, kd_ref, vd_ref, wide):
    heads, length, levels, block, bits = sizes
    base = block.bit_length() - 1
    for source, target in ((k_ref, kd_ref), (v_ref, vd_ref), (q_ref, qd_ref)):
        def store(head, value, target=target):
            target[head] = value.astype(BF16)
        split_heads(source, wide, heads, length, store)
    row = lax.broadcasted_iota(jnp.int32, (block, block), 0)
    column = lax.broadcasted_iota(jnp.int32, (block, block), 1)
    differs = row ^ column
    below = column <= row
    for head in range(heads):
        for i in range(length // block):
            rows = slice(i * block, (i + 1) * block)
            reach = slice(0, (i + 1) * block)
            def weight(level):
                return tw_ref[head, rows, level:level + 1]
            diagonal = jnp.broadcast_to(weight(0), (block, block))
            for level in range(1, base + 1):
                diagonal = jnp.where(differs >= 1 << (level - 1), weight(level), diagonal)
            diagonal = jnp.where(below, diagonal, 0.0)
            w_ref[head * (length // block) + i] = diagonal
            scores = dot(qd_ref[head, rows, :], kd_ref[head, reach, :], NT)
            parts = []
            for j in range(i):
                parts.append(scores[:, j * block:(j + 1) * block] * weight(base + (i ^ j).bit_length()))
            parts.append(scores[:, rows] * diagonal)
            for j, part in enumerate(parts):
                p_ref[head, rows, j * block:(j + 1) * block] = part.astype(BF16)
            inner_ref[head, rows, :] = dot(p_ref[head, rows, reach], vd_ref[head, reach, :], NN)


def cross_heads(sizes, heads_at, held_at, inner_ref, qd_ref, gg_ref, tw_ref, attn_ref, sums_ref, add=None):
    _, length, levels, block, bits = sizes
    for i in range(length // block):
        rows = slice(i * block, (i + 1) * block)
        squares = 0.0
        products = 0.0
        for h, head in enumerate(heads_at):
            total = inner_ref[head, rows, :]
            query = qd_ref[head, rows, :]
            for j in range(bits):
                at = levels - bits + j
                total = total + tw_ref[head, rows, at:at + 1] * dot(query, held_at(j, h), NN)
            attn_ref[h, rows, :] = total
            squares = squares + total * total
            products = products + total * gg_ref[head, rows, :]
        both = (squares, products)
        for n in range(2):
            row = jnp.sum(both[n].T, axis=0, keepdims=True)
            if add is not None:
                row = row + add[n:n + 1, rows]
            sums_ref[n:n + 1, rows] = row


def cross_mine(sizes, *refs):
    heads, length, levels, block, bits = sizes
    position_ref, inner_ref, qd_ref, gg_ref, tw_ref, near_ref = refs[:6]
    mine = refs[6:6 + bits - 1]
    attn_ref, sums_ref, held_ref = refs[-3:]
    half = heads // 2
    start = (position_ref[0] & 1) * half
    for h in range(half):
        held_ref[0, h] = near_ref[start + h].astype(BF16)
        for j in range(1, bits):
            held_ref[j, h] = mine[j - 1][h].astype(BF16)
    cross_heads(sizes, [start + h for h in range(half)], lambda j, h: held_ref[j, h],
                inner_ref, qd_ref, gg_ref, tw_ref, attn_ref, sums_ref)


def cross_other(sizes, *refs):
    heads, length, levels, block, bits = sizes
    position_ref, inner_ref, qd_ref, gg_ref, tw_ref, near_ref, add_ref = refs[:7]
    other = refs[7:7 + bits - 1]
    attn_ref, sums_ref, held_ref = refs[-3:]
    half = heads // 2
    start = (1 - (position_ref[0] & 1)) * half
    for h in range(half):
        held_ref[0, h] = near_ref[start + h].astype(BF16)
        for j in range(1, bits):
            held_ref[j, h] = other[j - 1][h].astype(BF16)
    cross_heads(sizes, [start + h for h in range(half)], lambda j, h: held_ref[j, h],
                inner_ref, qd_ref, gg_ref, tw_ref, attn_ref, sums_ref, add_ref)


def sibling(source, target, place):
    return ((source >> place) == (target >> place ^ 1)).astype(F32)


def combine_kernel(group, position_ref, *refs):
    far = group.bit_length() - 1
    received, targets = refs[:group - 1], refs[group - 1:]
    chip = (position_ref[0] >> 1) & (group - 1)
    for place in range(far):
        total = 0.0
        for step, block in zip(swaps(group), received):
            source = chip ^ step
            total = total + sibling(source, chip, place) * block[...]
        targets[place][...] = total


def message_kernel(group, position_ref, above_ref, keep_ref, came_ref, *targets):
    far = group.bit_length() - 1
    chip = (position_ref[0] >> 1) & (group - 1)
    for step, message in zip(swaps(group), targets):
        target = chip ^ step
        total = above_ref[...]
        for place in range(far):
            total = total + sibling(chip, target, place) * (keep_ref[place] + came_ref[place])
        message[...] = total


def spread(row, width):
    return jnp.broadcast_to(row, (width, row.shape[1])).T


def token_scales(features, sums):
    total = sums[0][...]
    for part in sums[1:]:
        total = total + part[...]
    inverse = lax.rsqrt(total[0:1] / features + epsilon)
    return inverse, inverse * inverse * inverse * (total[1:2] / features)


def grad_heads(sizes, heads_at, left_at, right_at, attn_ref, gg_ref, qd_ref, tw_ref, put_grad, scaled_ref, put_state):
    _, length, levels, block, bits = sizes
    width = attn_ref.shape[-1]
    for h, head in enumerate(heads_at):
        for i in range(length // block):
            rows = slice(i * block, (i + 1) * block)
            grad = (left_at(rows) * gg_ref[head, rows, :] - attn_ref[h, rows, :] * right_at(rows)).astype(BF16)
            put_grad(h, rows, grad)
            wide = grad.astype(F32)
            for j in range(bits):
                at = levels - bits + j
                scaled_ref[rows, j * width:(j + 1) * width] = (tw_ref[head, rows, at:at + 1] * wide).astype(BF16)
        product = dot(qd_ref[head], scaled_ref[...], TN)
        for j in range(bits):
            put_state(j, h, product[:, j * width:(j + 1) * width])


def grad_other(sizes, features, *refs):
    heads, length, levels, block, bits = sizes
    position_ref, attn_ref, gg_ref, qd_ref, tw_ref = refs[:5]
    sums = refs[5:-7]
    ag_ref, inverse_ref, left_ref, right_ref, first_ref, send_ref, scaled_ref = refs[-7:]
    half = heads // 2
    start = (1 - (position_ref[0] & 1)) * half
    width = attn_ref.shape[-1]
    inverse, beta = token_scales(features, sums)
    inverse_ref[...] = inverse
    for i in range(length // block):
        rows = slice(i * block, (i + 1) * block)
        left_ref[rows, :] = spread(inverse[:, rows], width)
        right_ref[rows, :] = spread(beta[:, rows], width)

    def put_grad(h, rows, grad):
        ag_ref[h, rows, :] = grad

    def put_state(j, h, value):
        if j == 0:
            first_ref[h] = value
        else:
            send_ref[j - 1, h] = value
    grad_heads(sizes, [start + h for h in range(half)], lambda rows: left_ref[rows, :], lambda rows: right_ref[rows, :],
               attn_ref, gg_ref, qd_ref, tw_ref, put_grad, scaled_ref, put_state)


def grad_mine(sizes, position_ref, attn_ref, far_ref, gg_ref, qd_ref, tw_ref, other_ref, left_ref, right_ref,
              held_mine_ref, held_other_ref, ag_ref, first_ref, keep_ref, attn_full_ref, held_ref, scaled_ref):
    heads, length, levels, block, bits = sizes
    half = heads // 2
    core = position_ref[0] & 1
    start = core * half
    away = (1 - core) * half

    def put_grad(h, rows, grad):
        ag_ref[start + h, rows, :] = grad

    def put_state(j, h, value):
        if j == 0:
            first_ref[h] = value
        else:
            keep_ref[j - 1, h] = value
    grad_heads(sizes, [start + h for h in range(half)], lambda rows: left_ref[rows, :], lambda rows: right_ref[rows, :],
               attn_ref, gg_ref, qd_ref, tw_ref, put_grad, scaled_ref, put_state)
    for h in range(half):
        ag_ref[away + h] = other_ref[h]
        attn_full_ref[start + h] = attn_ref[h]
        attn_full_ref[away + h] = far_ref[h]
        for j in range(bits):
            held_ref[j, start + h] = held_mine_ref[j, h]
            held_ref[j, away + h] = held_other_ref[j, h]


def local_backward(sizes, ag_ref, qd_ref, kd_ref, vd_ref, p_ref, w_ref, tw_ref, held_ref, attn_ref,
                   inverse_ref, gain_ref, normed_ref, dq_ref, dk_ref, dv_ref, weighted_ref):
    heads, length, levels, block, bits = sizes
    base = block.bit_length() - 1
    width = ag_ref.shape[-1]
    blocks = length // block
    for i in range(blocks):
        rows = slice(i * block, (i + 1) * block)
        reach = slice(0, (i + 1) * block)
        left = spread(inverse_ref[:, rows], width)
        for head in range(heads):
            put = pl.ds(i * block * heads + head, block, stride=heads)
            normed_ref[put, :] = attn_ref[head, rows, :] * left * gain_ref[head:head + 1, :]
            def weight(level):
                return tw_ref[head, rows, level:level + 1]
            grad = ag_ref[head, rows, :]
            scores = dot(grad, vd_ref[head, reach, :], NT)
            for j in range(i + 1):
                part = scores[:, j * block:(j + 1) * block]
                if j == i:
                    part = part * w_ref[head * blocks + i]
                else:
                    part = part * weight(base + (i ^ j).bit_length())
                weighted_ref[head, rows, j * block:(j + 1) * block] = part.astype(BF16)
            total = dot(weighted_ref[head, rows, reach], kd_ref[head, reach, :], NN)
            for j in range(bits):
                total = total + weight(levels - bits + j) * dot(grad, held_ref[j, head], NT)
            dq_ref[put, :] = total
    for head in range(heads):
        for j in range(blocks):
            cols = slice(j * block, (j + 1) * block)
            rest = slice(j * block, length)
            dk_ref[head, cols, :] = dot(weighted_ref[head, rest, cols], qd_ref[head, rest, :], TN)
            dv_ref[head, cols, :] = dot(p_ref[head, rest, cols], ag_ref[head, rest, :], TN)


def final_heads(sizes, start, position_ref, near_ref, total_ref, kd_ref, vd_ref, dk_ref, dv_ref,
                key_ref, value_ref, key_hbm, value_hbm, sems):
    heads, length, block = sizes
    half = heads // 2
    keep = (1 - (position_ref[0] & 1)).astype(F32)
    copies = []
    for h in range(half):
        head = start + h
        back = (total_ref[h] + keep * near_ref[h]).astype(BF16)
        key_ref[h] = dk_ref[head] + dot(vd_ref[head], back, NT)
        copies.append(pltpu.make_async_copy(key_ref.at[h], key_hbm.at[:, head, :], sems.at[0, h]))
        copies[-1].start()
        value_ref[h] = dv_ref[head] + dot(kd_ref[head], back, NN)
        copies.append(pltpu.make_async_copy(value_ref.at[h], value_hbm.at[:, head, :], sems.at[1, h]))
        copies[-1].start()
    for copy in copies:
        copy.wait()


def final_mine(sizes, position_ref, *refs):
    final_heads(sizes, (position_ref[0] & 1) * (sizes[0] // 2), position_ref, *refs[:6], *refs[8:10], *refs[6:8], refs[10])


def final_other(sizes, position_ref, *refs):
    start = (1 - (position_ref[0] & 1)) * (sizes[0] // 2)
    final_heads(sizes, start, position_ref, *refs[:6], *refs[10:12], *refs[8:10], refs[12])


def shards(query_rows, key_rows, value_rows, level_pick, level_table, norm_gain, out_grad):
    length, heads, width = query_rows.shape
    groups, _, levels = level_table.shape
    local_bits = length.bit_length() - 1
    bits = lax.axis_size("seq").bit_length() - 1
    block = min(128, length)
    half = heads // 2
    scale = width ** (-0.5)
    position = lax.axis_index("seq").astype(jnp.int32)
    place_arg = position.reshape(1)
    shape = jax.ShapeDtypeStruct

    own = jnp.einsum("shd,she->hde", key_rows, value_rows, preferred_element_type=F32)
    near = swapped(own, "seq", 0)
    sizes = (heads, length, levels, block, bits)
    rows = length * heads
    flat = lambda a: a.reshape(rows, width)
    local_flops = heads * length * length * width
    weights = call(
        functools.partial(level_rows, sizes, scale),
        shape((heads, length, levels), F32),
        (place_arg, level_pick.reshape(1, length), level_table),
        [SMEM, VMEM, VMEM],
        name="level_rows",
    )
    pair = own + near

    block_sum = lax.dynamic_slice(
        pair, ((position & 1) * half, 0, 0), (half, width, width), allow_negative_indices=False
    )
    far = min(bits - 1, 2)
    group = 1 << far
    received = turned([block_sum] * (group - 1), "seq", group)

    inner, probs, diag, qd, kd, vd = call(
        functools.partial(local_forward, sizes),
        (
            shape((heads, length, width), F32),
            shape((heads, length, length), BF16),
            shape((heads * (length // block), block, block), F32),
            shape((heads, length, width), BF16),
            shape((heads, length, width), BF16),
            shape((heads, length, width), BF16),
        ),
        (flat(query_rows), flat(key_rows), flat(value_rows), weights),
        [VMEM] * 4,
        [pltpu.VMEM((rows, width), F32)],
        flops=4 * local_flops,
        name="local_forward",
    )
    gg = call(
        functools.partial(gain_rows, (heads, length)),
        shape((heads, length, width), F32),
        (flat(out_grad), norm_gain),
        [VMEM] * 2,
        [pltpu.VMEM((rows, width), F32)],
        name="gain_rows",
    )
    inner, gg, received = lax.optimization_barrier((inner, gg, received))
    state = shape((half, width, width), F32)
    mine = call(
        functools.partial(combine_kernel, group),
        (state,) * far,
        (place_arg, *received),
        [SMEM] + [VMEM] * (group - 1),
        name="far_states",
    )
    mine = list(mine)
    block_sum = functools.reduce(jnp.add, received, block_sum)
    for place in range(far + 1, bits):
        mine.append(swapped(block_sum, "seq", place))
        block_sum = block_sum + mine[-1]
    others = [swapped(partner, "seq", 0) for partner in mine]
    cross_flops = bits * heads * length * width * width
    cross_shapes = (
        shape((half, length, width), F32),
        shape((2, length), F32),
        shape((bits, half, width, width), BF16),
    )
    attn_mine, sums, held_mine = call(
        functools.partial(cross_mine, sizes),
        cross_shapes,
        (place_arg, inner, qd, gg, weights, near, *mine),
        [SMEM] + [VMEM] * (5 + len(mine)),
        flops=cross_flops,
        name="cross_mine",
    )
    attn_other, sums, held_other = call(
        functools.partial(cross_other, sizes),
        cross_shapes,
        (place_arg, inner, qd, gg, weights, near, sums, *others),
        [SMEM] + [VMEM] * (6 + len(others)),
        flops=cross_flops,
        name="cross_other",
    )
    features = heads * width * lax.axis_size("heads")
    parts = summands(sums, "heads")
    grad_far, inverse, left, right, first_other, send = call(
        functools.partial(grad_other, sizes, features),
        (
            shape((half, length, width), BF16),
            shape((1, length), F32),
            shape((length, width), F32),
            shape((length, width), F32),
            shape((half, width, width), F32),
            shape((bits - 1, half, width, width), F32),
        ),
        (place_arg, attn_other, gg, qd, weights, *parts),
        [SMEM] + [VMEM] * (4 + len(parts)),
        [pltpu.VMEM((length, bits * width), BF16)],
        flops=cross_flops,
        name="state_grads_other",
    )
    attn_grad, first_mine, keep, attn, held = call(
        functools.partial(grad_mine, sizes),
        (
            shape((heads, length, width), BF16),
            shape((half, width, width), F32),
            shape((bits - 1, half, width, width), F32),
            shape((heads, length, width), F32),
            shape((bits, heads, width, width), BF16),
        ),
        (place_arg, attn_mine, attn_other, gg, qd, weights, grad_far, left, right, held_mine, held_other),
        [SMEM] + [VMEM] * 10,
        [pltpu.VMEM((length, bits * width), BF16)],
        flops=cross_flops,
        name="state_grads_mine",
    )
    came = swapped(send, "seq", 0)
    above = jnp.zeros((half, width, width), F32)
    for place in reversed(range(far + 1, bits)):
        above = above + swapped(above + keep[place - 1] + came[place - 1], "seq", place)
    messages = call(
        functools.partial(message_kernel, group),
        (state,) * (group - 1),
        (place_arg, above, keep, came),
        [SMEM] + [VMEM] * 3,
        name="far_messages",
    )
    landed = turned(messages, "seq", group)
    near_other = swapped(first_mine, "seq", 0)
    near_mine = swapped(first_other, "seq", 0)

    normed, query_grad, key_part, value_part = call(
        functools.partial(local_backward, sizes),
        (
            shape((rows, width), F32),
            shape((rows, width), F32),
            shape((heads, length, width), F32),
            shape((heads, length, width), F32),
        ),
        (attn_grad, qd, kd, vd, probs, diag, weights, held, attn, inverse, norm_gain),
        [VMEM] * 11,
        [pltpu.VMEM((heads, length, length), BF16)],
        flops=8 * local_flops,
        name="local_backward",
    )
    landed, key_part = lax.optimization_barrier((landed, key_part))
    total = functools.reduce(jnp.add, landed, above)
    other = swapped(total, "seq", 0)

    final_sizes = (heads, length, block)
    final_flops = 2 * heads * length * width * width
    whole = (shape((length, heads, width), F32), shape((length, heads, width), F32))
    scratch = [
        pltpu.VMEM((half, length, width), F32),
        pltpu.VMEM((half, length, width), F32),
        pltpu.SemaphoreType.DMA((2, half)),
    ]
    started = call(
        functools.partial(final_mine, final_sizes),
        whole,
        (place_arg, near_mine, total, kd, vd, key_part, value_part),
        [SMEM] + [VMEM] * 6,
        scratch,
        flops=final_flops,
        name="key_value_mine",
        outs=HBM,
    )
    key_grad, value_grad = call(
        functools.partial(final_other, final_sizes),
        whole,
        (place_arg, near_other, other, kd, vd, key_part, value_part, *started),
        [SMEM] + [VMEM] * 6 + [HBM] * 2,
        scratch,
        flops=final_flops,
        name="key_value_other",
        outs=HBM,
        aliases={7: 0, 8: 1},
    )
    return tuple(a.reshape(length, heads, width) for a in (normed, query_grad, key_grad, value_grad))


def solution(mesh):
    in_specs = (
        P("seq", "heads", None),
        P("seq", "heads", None),
        P("seq", "heads", None),
        P("seq"),
        P(None, "heads", None),
        P("heads", None),
        P("seq", "heads", None),
    )
    out_specs = (
        P("seq", "heads", None),
        P("seq", "heads", None),
        P("seq", "heads", None),
        P("seq", "heads", None),
    )
    return jax.shard_map(shards, mesh=mesh, in_specs=in_specs, out_specs=out_specs, check_vma=False)
```

```python
import functools

import jax
import jax.numpy as jnp
from jax import lax
from jax.experimental import pallas as pl
from jax.experimental.pallas import tpu as pltpu
from jax.sharding import PartitionSpec as P

exact_mode = lax.Precision.HIGHEST
epsilon = 1e-06
F32 = jnp.float32
BF16 = jnp.bfloat16
VMEM = pl.BlockSpec(memory_space=pltpu.VMEM)
HBM = pl.BlockSpec(memory_space=pltpu.HBM)
SMEM = pl.BlockSpec(memory_space=pltpu.SMEM)
NT = (((1,), (1,)), ((), ()))
TN = (((0,), (0,)), ((), ()))
NN = (((1,), (0,)), ((), ()))


def dot(left, right, dims):
    return lax.dot_general(left, right, dims, preferred_element_type=F32)


def swapped(block, axis, distance):
    count = lax.axis_size(axis)
    route = []
    for low in range(count):
        high = low | 1 << distance
        if high != low and high < count:
            route += [(low, high), (high, low)]
    return lax.ppermute(block, axis, route)


def turns(count):
    order = []
    for step in range(1, count // 2 + 1):
        order += [step] if 2 * step == count else [step, count - step]
    return order


def swaps(group):
    return list(range(group - 1, 0, -1))


def summands(block, axis):
    count = lax.axis_size(axis)
    result = [block]
    for step in turns(count):
        result.append(lax.ppermute(block, axis, [(i, (i + step) % count) for i in range(count)]))
    return result


def turned(blocks, axis, group):
    count = lax.axis_size(axis)
    result = []
    for step, block in zip(swaps(group), blocks):
        route = []
        for i in range(count):
            chip = i >> 1
            target = chip - chip % group + (chip % group ^ step)
            route.append((i, target << 1 | i & 1))
        result.append(lax.ppermute(block, axis, route))
    return result


def call(kernel, out_shape, args, specs, scratch=(), flops=0, name=None, outs=VMEM, aliases={}):
    return pl.pallas_call(
        kernel,
        out_shape=out_shape,
        in_specs=specs,
        out_specs=jax.tree.map(lambda _: outs, out_shape),
        scratch_shapes=list(scratch),
        compiler_params=pltpu.CompilerParams(vmem_limit_bytes=16 << 20),
        cost_estimate=pl.CostEstimate(
            flops=flops,
            transcendentals=0,
            bytes_accessed=sum(a.size * a.dtype.itemsize for a in args),
        ),
        name=name,
        input_output_aliases=aliases,
    )(*args)


def split_heads(source, wide, heads, length, store):
    wide[...] = source[...].astype(F32)
    for head in range(heads):
        store(head, wide[pl.ds(head, length, stride=heads), :])


def level_rows(sizes, scale, position_ref, pick_ref, table_ref, tw_ref):
    heads, length, levels, block, bits = sizes
    groups = table_ref.shape[0]
    lane = lax.broadcasted_iota(jnp.int32, (groups, levels), 1)
    factor = jnp.full((groups, levels), scale, F32)
    for j in range(bits):
        flag = (position_ref[0] >> j & 1).astype(F32) * scale
        factor = jnp.where(lane == levels - bits + j, flag, factor)
    group = lax.broadcasted_iota(jnp.int32, (groups, length), 0)
    one_hot = (group == pick_ref[...]).astype(F32)
    for head in range(heads):
        table = table_ref[:, head, :] * factor
        tw_ref[head] = lax.dot_general(one_hot, table, TN, precision=exact_mode, preferred_element_type=F32)


def gain_rows(sizes, g_ref, gain_ref, gg_ref, wide):
    heads, length = sizes

    def store(head, value):
        gg_ref[head] = value * gain_ref[head:head + 1, :]
    split_heads(g_ref, wide, heads, length, store)


def local_forward(sizes, q_ref, k_ref, v_ref, tw_ref, inner_ref, p_ref, w_ref, qd_ref, kd_ref, vd_ref, wide):
    heads, length, levels, block, bits = sizes
    base = block.bit_length() - 1
    for source, target in ((k_ref, kd_ref), (v_ref, vd_ref), (q_ref, qd_ref)):
        def store(head, value, target=target):
            target[head] = value.astype(BF16)
        split_heads(source, wide, heads, length, store)
    row = lax.broadcasted_iota(jnp.int32, (block, block), 0)
    column = lax.broadcasted_iota(jnp.int32, (block, block), 1)
    differs = row ^ column
    below = column <= row
    for head in range(heads):
        for i in range(length // block):
            rows = slice(i * block, (i + 1) * block)
            reach = slice(0, (i + 1) * block)
            def weight(level):
                return tw_ref[head, rows, level:level + 1]
            diagonal = jnp.broadcast_to(weight(0), (block, block))
            for level in range(1, base + 1):
                diagonal = jnp.where(differs >= 1 << (level - 1), weight(level), diagonal)
            diagonal = jnp.where(below, diagonal, 0.0)
            w_ref[head * (length // block) + i] = diagonal
            scores = dot(qd_ref[head, rows, :], kd_ref[head, reach, :], NT)
            parts = []
            for j in range(i):
                parts.append(scores[:, j * block:(j + 1) * block] * weight(base + (i ^ j).bit_length()))
            parts.append(scores[:, rows] * diagonal)
            for j, part in enumerate(parts):
                p_ref[head, rows, j * block:(j + 1) * block] = part.astype(BF16)
            inner_ref[head, rows, :] = dot(p_ref[head, rows, reach], vd_ref[head, reach, :], NN)


def cross_heads(sizes, heads_at, held_at, inner_ref, qd_ref, gg_ref, tw_ref, attn_ref, sums_ref, add=None):
    _, length, levels, block, bits = sizes
    for i in range(length // block):
        rows = slice(i * block, (i + 1) * block)
        squares = 0.0
        products = 0.0
        for h, head in enumerate(heads_at):
            total = inner_ref[head, rows, :]
            query = qd_ref[head, rows, :]
            for j in range(bits):
                at = levels - bits + j
                total = total + tw_ref[head, rows, at:at + 1] * dot(query, held_at(j, h), NN)
            attn_ref[h, rows, :] = total
            squares = squares + total * total
            products = products + total * gg_ref[head, rows, :]
        both = (squares, products)
        for n in range(2):
            row = jnp.sum(both[n].T, axis=0, keepdims=True)
            if add is not None:
                row = row + add[n:n + 1, rows]
            sums_ref[n:n + 1, rows] = row


def cross_mine(sizes, *refs):
    heads, length, levels, block, bits = sizes
    position_ref, inner_ref, qd_ref, gg_ref, tw_ref, near_ref = refs[:6]
    mine = refs[6:6 + bits - 1]
    attn_ref, sums_ref, held_ref = refs[-3:]
    half = heads // 2
    start = (position_ref[0] & 1) * half
    for h in range(half):
        held_ref[0, h] = near_ref[start + h].astype(BF16)
        for j in range(1, bits):
            held_ref[j, h] = mine[j - 1][h].astype(BF16)
    cross_heads(sizes, [start + h for h in range(half)], lambda j, h: held_ref[j, h],
                inner_ref, qd_ref, gg_ref, tw_ref, attn_ref, sums_ref)


def cross_other(sizes, *refs):
    heads, length, levels, block, bits = sizes
    position_ref, inner_ref, qd_ref, gg_ref, tw_ref, near_ref, add_ref = refs[:7]
    other = refs[7:7 + bits - 1]
    attn_ref, sums_ref, held_ref = refs[-3:]
    half = heads // 2
    start = (1 - (position_ref[0] & 1)) * half
    for h in range(half):
        held_ref[0, h] = near_ref[start + h].astype(BF16)
        for j in range(1, bits):
            held_ref[j, h] = other[j - 1][h].astype(BF16)
    cross_heads(sizes, [start + h for h in range(half)], lambda j, h: held_ref[j, h],
                inner_ref, qd_ref, gg_ref, tw_ref, attn_ref, sums_ref, add_ref)


def sibling(source, target, place):
    return ((source >> place) == (target >> place ^ 1)).astype(F32)


def combine_kernel(group, position_ref, *refs):
    far = group.bit_length() - 1
    received, targets = refs[:group - 1], refs[group - 1:]
    chip = (position_ref[0] >> 1) & (group - 1)
    for place in range(far):
        total = 0.0
        for step, block in zip(swaps(group), received):
            source = chip ^ step
            total = total + sibling(source, chip, place) * block[...]
        targets[place][...] = total


def message_kernel(group, position_ref, above_ref, keep_ref, came_ref, *targets):
    far = group.bit_length() - 1
    chip = (position_ref[0] >> 1) & (group - 1)
    for step, message in zip(swaps(group), targets):
        target = chip ^ step
        total = above_ref[...]
        for place in range(far):
            total = total + sibling(chip, target, place) * (keep_ref[place] + came_ref[place])
        message[...] = total


def spread(row, width):
    return jnp.broadcast_to(row, (width, row.shape[1])).T


def token_scales(features, sums):
    total = sums[0][...]
    for part in sums[1:]:
        total = total + part[...]
    inverse = lax.rsqrt(total[0:1] / features + epsilon)
    return inverse, inverse * inverse * inverse * (total[1:2] / features)


def grad_heads(sizes, heads_at, left_at, right_at, attn_ref, gg_ref, qd_ref, tw_ref, put_grad, scaled_ref, put_state, lowest=0):
    _, length, levels, block, bits = sizes
    width = attn_ref.shape[-1]
    for h, head in enumerate(heads_at):
        for i in range(length // block):
            rows = slice(i * block, (i + 1) * block)
            grad = (left_at(rows) * gg_ref[head, rows, :] - attn_ref[h, rows, :] * right_at(rows)).astype(BF16)
            put_grad(h, rows, grad)
            wide = grad.astype(F32)
            for j in range(lowest, bits):
                at = levels - bits + j
                scaled_ref[rows, (j - lowest) * width:(j - lowest + 1) * width] = (tw_ref[head, rows, at:at + 1] * wide).astype(BF16)
        product = dot(qd_ref[head], scaled_ref[:, :(bits - lowest) * width], TN)
        for j in range(lowest, bits):
            put_state(j, h, product[:, (j - lowest) * width:(j - lowest + 1) * width])


def grad_other(sizes, features, *refs):
    heads, length, levels, block, bits = sizes
    position_ref, attn_ref, gg_ref, qd_ref, tw_ref = refs[:5]
    sums = refs[5:-6]
    ag_ref, inverse_ref, left_ref, right_ref, send_ref, scaled_ref = refs[-6:]
    half = heads // 2
    start = (1 - (position_ref[0] & 1)) * half
    width = attn_ref.shape[-1]
    inverse, beta = token_scales(features, sums)
    inverse_ref[...] = inverse
    for i in range(length // block):
        rows = slice(i * block, (i + 1) * block)
        left_ref[rows, :] = spread(inverse[:, rows], width)
        right_ref[rows, :] = spread(beta[:, rows], width)

    def put_grad(h, rows, grad):
        ag_ref[h, rows, :] = grad

    def put_state(j, h, value):
        send_ref[j - 1, h] = value
    grad_heads(sizes, [start + h for h in range(half)], lambda rows: left_ref[rows, :], lambda rows: right_ref[rows, :],
               attn_ref, gg_ref, qd_ref, tw_ref, put_grad, scaled_ref, put_state, 1)


def grad_mine(sizes, position_ref, attn_ref, far_ref, gg_ref, qd_ref, tw_ref, other_ref, left_ref, right_ref,
              held_mine_ref, held_other_ref, ag_ref, first_ref, first_far_ref, keep_ref, attn_full_ref, held_ref, scaled_ref):
    heads, length, levels, block, bits = sizes
    half = heads // 2
    core = position_ref[0] & 1
    start = core * half
    away = (1 - core) * half

    def put_grad(h, rows, grad):
        ag_ref[start + h, rows, :] = grad

    def put_state(j, h, value):
        if j == 0:
            first_ref[h] = value
        else:
            keep_ref[j - 1, h] = value
    grad_heads(sizes, [start + h for h in range(half)], lambda rows: left_ref[rows, :], lambda rows: right_ref[rows, :],
               attn_ref, gg_ref, qd_ref, tw_ref, put_grad, scaled_ref, put_state)
    for h in range(half):
        ag_ref[away + h] = other_ref[h]
        at = levels - bits
        width = other_ref.shape[-1]
        scaled_ref[:, :width] = (tw_ref[away + h, :, at:at + 1] * other_ref[h].astype(F32)).astype(BF16)
        first_far_ref[h] = dot(qd_ref[away + h], scaled_ref[:, :width], TN)
        attn_full_ref[start + h] = attn_ref[h]
        attn_full_ref[away + h] = far_ref[h]
        for j in range(bits):
            held_ref[j, start + h] = held_mine_ref[j, h]
            held_ref[j, away + h] = held_other_ref[j, h]


def local_backward(sizes, ag_ref, qd_ref, kd_ref, vd_ref, p_ref, w_ref, tw_ref, held_ref, attn_ref,
                   inverse_ref, gain_ref, normed_ref, dq_ref, dk_ref, dv_ref, weighted_ref):
    heads, length, levels, block, bits = sizes
    base = block.bit_length() - 1
    width = ag_ref.shape[-1]
    blocks = length // block
    for i in range(blocks):
        rows = slice(i * block, (i + 1) * block)
        reach = slice(0, (i + 1) * block)
        left = spread(inverse_ref[:, rows], width)
        for head in range(heads):
            put = pl.ds(i * block * heads + head, block, stride=heads)
            normed_ref[put, :] = attn_ref[head, rows, :] * left * gain_ref[head:head + 1, :]
            def weight(level):
                return tw_ref[head, rows, level:level + 1]
            grad = ag_ref[head, rows, :]
            scores = dot(grad, vd_ref[head, reach, :], NT)
            for j in range(i + 1):
                part = scores[:, j * block:(j + 1) * block]
                if j == i:
                    part = part * w_ref[head * blocks + i]
                else:
                    part = part * weight(base + (i ^ j).bit_length())
                weighted_ref[head, rows, j * block:(j + 1) * block] = part.astype(BF16)
            total = dot(weighted_ref[head, rows, reach], kd_ref[head, reach, :], NN)
            for j in range(bits):
                total = total + weight(levels - bits + j) * dot(grad, held_ref[j, head], NT)
            dq_ref[put, :] = total
    for head in range(heads):
        for j in range(blocks):
            cols = slice(j * block, (j + 1) * block)
            rest = slice(j * block, length)
            dk_ref[head, cols, :] = dot(weighted_ref[head, rest, cols], qd_ref[head, rest, :], TN)
            dv_ref[head, cols, :] = dot(p_ref[head, rest, cols], ag_ref[head, rest, :], TN)


def final_heads(sizes, start, position_ref, near_ref, total_ref, kd_ref, vd_ref, dk_ref, dv_ref,
                key_ref, value_ref, key_hbm, value_hbm, sems):
    heads, length, block = sizes
    half = heads // 2
    keep = (1 - (position_ref[0] & 1)).astype(F32)
    copies = []
    for h in range(half):
        head = start + h
        back = (total_ref[h] + keep * near_ref[h]).astype(BF16)
        key_ref[h] = dk_ref[head] + dot(vd_ref[head], back, NT)
        copies.append(pltpu.make_async_copy(key_ref.at[h], key_hbm.at[:, head, :], sems.at[0, h]))
        copies[-1].start()
        value_ref[h] = dv_ref[head] + dot(kd_ref[head], back, NN)
        copies.append(pltpu.make_async_copy(value_ref.at[h], value_hbm.at[:, head, :], sems.at[1, h]))
        copies[-1].start()
    for copy in copies:
        copy.wait()


def final_mine(sizes, position_ref, *refs):
    final_heads(sizes, (position_ref[0] & 1) * (sizes[0] // 2), position_ref, *refs[:6], *refs[8:10], *refs[6:8], refs[10])


def final_other(sizes, position_ref, *refs):
    start = (1 - (position_ref[0] & 1)) * (sizes[0] // 2)
    final_heads(sizes, start, position_ref, *refs[:6], *refs[10:12], *refs[8:10], refs[12])


def shards(query_rows, key_rows, value_rows, level_pick, level_table, norm_gain, out_grad):
    length, heads, width = query_rows.shape
    groups, _, levels = level_table.shape
    local_bits = length.bit_length() - 1
    bits = lax.axis_size("seq").bit_length() - 1
    block = min(128, length)
    half = heads // 2
    scale = width ** (-0.5)
    position = lax.axis_index("seq").astype(jnp.int32)
    place_arg = position.reshape(1)
    shape = jax.ShapeDtypeStruct

    own = jnp.einsum("shd,she->hde", key_rows, value_rows, preferred_element_type=F32)
    near = swapped(own, "seq", 0)
    sizes = (heads, length, levels, block, bits)
    rows = length * heads
    flat = lambda a: a.reshape(rows, width)
    local_flops = heads * length * length * width
    weights = call(
        functools.partial(level_rows, sizes, scale),
        shape((heads, length, levels), F32),
        (place_arg, level_pick.reshape(1, length), level_table),
        [SMEM, VMEM, VMEM],
        name="level_rows",
    )
    pair = own + near

    block_sum = lax.dynamic_slice(
        pair, ((position & 1) * half, 0, 0), (half, width, width), allow_negative_indices=False
    )
    far = min(bits - 1, 2)
    group = 1 << far
    received = turned([block_sum] * (group - 1), "seq", group)

    inner, probs, diag, qd, kd, vd = call(
        functools.partial(local_forward, sizes),
        (
            shape((heads, length, width), F32),
            shape((heads, length, length), BF16),
            shape((heads * (length // block), block, block), F32),
            shape((heads, length, width), BF16),
            shape((heads, length, width), BF16),
            shape((heads, length, width), BF16),
        ),
        (flat(query_rows), flat(key_rows), flat(value_rows), weights),
        [VMEM] * 4,
        [pltpu.VMEM((rows, width), F32)],
        flops=4 * local_flops,
        name="local_forward",
    )
    gg = call(
        functools.partial(gain_rows, (heads, length)),
        shape((heads, length, width), F32),
        (flat(out_grad), norm_gain),
        [VMEM] * 2,
        [pltpu.VMEM((rows, width), F32)],
        name="gain_rows",
    )
    inner, gg, received = lax.optimization_barrier((inner, gg, received))
    state = shape((half, width, width), F32)
    mine = call(
        functools.partial(combine_kernel, group),
        (state,) * far,
        (place_arg, *received),
        [SMEM] + [VMEM] * (group - 1),
        name="far_states",
    )
    mine = list(mine)
    block_sum = functools.reduce(jnp.add, received, block_sum)
    for place in range(far + 1, bits):
        mine.append(swapped(block_sum, "seq", place))
        block_sum = block_sum + mine[-1]
    others = [swapped(partner, "seq", 0) for partner in mine]
    cross_flops = bits * heads * length * width * width
    cross_shapes = (
        shape((half, length, width), F32),
        shape((2, length), F32),
        shape((bits, half, width, width), BF16),
    )
    attn_mine, sums, held_mine = call(
        functools.partial(cross_mine, sizes),
        cross_shapes,
        (place_arg, inner, qd, gg, weights, near, *mine),
        [SMEM] + [VMEM] * (5 + len(mine)),
        flops=cross_flops,
        name="cross_mine",
    )
    attn_other, sums, held_other = call(
        functools.partial(cross_other, sizes),
        cross_shapes,
        (place_arg, inner, qd, gg, weights, near, sums, *others),
        [SMEM] + [VMEM] * (6 + len(others)),
        flops=cross_flops,
        name="cross_other",
    )
    features = heads * width * lax.axis_size("heads")
    parts = summands(sums, "heads")
    grad_far, inverse, left, right, send = call(
        functools.partial(grad_other, sizes, features),
        (
            shape((half, length, width), BF16),
            shape((1, length), F32),
            shape((length, width), F32),
            shape((length, width), F32),
            shape((bits - 1, half, width, width), F32),
        ),
        (place_arg, attn_other, gg, qd, weights, *parts),
        [SMEM] + [VMEM] * (4 + len(parts)),
        [pltpu.VMEM((length, bits * width), BF16)],
        flops=cross_flops,
        name="state_grads_other",
    )
    attn_grad, first_mine, first_other, keep, attn, held = call(
        functools.partial(grad_mine, sizes),
        (
            shape((heads, length, width), BF16),
            shape((half, width, width), F32),
            shape((half, width, width), F32),
            shape((bits - 1, half, width, width), F32),
            shape((heads, length, width), F32),
            shape((bits, heads, width, width), BF16),
        ),
        (place_arg, attn_mine, attn_other, gg, qd, weights, grad_far, left, right, held_mine, held_other),
        [SMEM] + [VMEM] * 10,
        [pltpu.VMEM((length, bits * width), BF16)],
        flops=cross_flops,
        name="state_grads_mine",
    )
    came = swapped(send, "seq", 0)
    above = jnp.zeros((half, width, width), F32)
    for place in reversed(range(far + 1, bits)):
        above = above + swapped(above + keep[place - 1] + came[place - 1], "seq", place)
    messages = call(
        functools.partial(message_kernel, group),
        (state,) * (group - 1),
        (place_arg, above, keep, came),
        [SMEM] + [VMEM] * 3,
        name="far_messages",
    )
    landed = turned(messages, "seq", group)
    near_other = swapped(first_mine, "seq", 0)
    near_mine = swapped(first_other, "seq", 0)

    normed, query_grad, key_part, value_part = call(
        functools.partial(local_backward, sizes),
        (
            shape((rows, width), F32),
            shape((rows, width), F32),
            shape((heads, length, width), F32),
            shape((heads, length, width), F32),
        ),
        (attn_grad, qd, kd, vd, probs, diag, weights, held, attn, inverse, norm_gain),
        [VMEM] * 11,
        [pltpu.VMEM((heads, length, length), BF16)],
        flops=8 * local_flops,
        name="local_backward",
    )
    landed, key_part = lax.optimization_barrier((landed, key_part))
    total = functools.reduce(jnp.add, landed, above)
    other = swapped(total, "seq", 0)

    final_sizes = (heads, length, block)
    final_flops = 2 * heads * length * width * width
    whole = (shape((length, heads, width), F32), shape((length, heads, width), F32))
    scratch = [
        pltpu.VMEM((half, length, width), F32),
        pltpu.VMEM((half, length, width), F32),
        pltpu.SemaphoreType.DMA((2, half)),
    ]
    started = call(
        functools.partial(final_mine, final_sizes),
        whole,
        (place_arg, near_mine, total, kd, vd, key_part, value_part),
        [SMEM] + [VMEM] * 6,
        scratch,
        flops=final_flops,
        name="key_value_mine",
        outs=HBM,
    )
    key_grad, value_grad = call(
        functools.partial(final_other, final_sizes),
        whole,
        (place_arg, near_other, other, kd, vd, key_part, value_part, *started),
        [SMEM] + [VMEM] * 6 + [HBM] * 2,
        scratch,
        flops=final_flops,
        name="key_value_other",
        outs=HBM,
        aliases={7: 0, 8: 1},
    )
    return tuple(a.reshape(length, heads, width) for a in (normed, query_grad, key_grad, value_grad))


def solution(mesh):
    in_specs = (
        P("seq", "heads", None),
        P("seq", "heads", None),
        P("seq", "heads", None),
        P("seq"),
        P(None, "heads", None),
        P("heads", None),
        P("seq", "heads", None),
    )
    out_specs = (
        P("seq", "heads", None),
        P("seq", "heads", None),
        P("seq", "heads", None),
        P("seq", "heads", None),
    )
    return jax.shard_map(shards, mesh=mesh, in_specs=in_specs, out_specs=out_specs, check_vma=False)
```

```python
import functools

import jax
import jax.numpy as jnp
from jax import lax
from jax.experimental import pallas as pl
from jax.experimental.pallas import tpu as pltpu
from jax.sharding import PartitionSpec as P

exact_mode = lax.Precision.HIGHEST
epsilon = 1e-06
F32 = jnp.float32
BF16 = jnp.bfloat16
VMEM = pl.BlockSpec(memory_space=pltpu.VMEM)
HBM = pl.BlockSpec(memory_space=pltpu.HBM)
SMEM = pl.BlockSpec(memory_space=pltpu.SMEM)
NT = (((1,), (1,)), ((), ()))
TN = (((0,), (0,)), ((), ()))
NN = (((1,), (0,)), ((), ()))


def dot(left, right, dims):
    return lax.dot_general(left, right, dims, preferred_element_type=F32)


def swapped(block, axis, distance):
    count = lax.axis_size(axis)
    route = []
    for low in range(count):
        high = low | 1 << distance
        if high != low and high < count:
            route += [(low, high), (high, low)]
    return lax.ppermute(block, axis, route)


def turns(count):
    order = []
    for step in range(1, count // 2 + 1):
        order += [step] if 2 * step == count else [step, count - step]
    return order


def swaps(group):
    return list(range(group - 1, 0, -1))


def back_swaps(group):
    return [group - 1, *range(1, group - 1)]


def summands(block, axis):
    count = lax.axis_size(axis)
    result = [block]
    for step in turns(count):
        result.append(lax.ppermute(block, axis, [(i, (i + step) % count) for i in range(count)]))
    return result


def turned(blocks, axis, group, order):
    count = lax.axis_size(axis)
    result = []
    for step, block in zip(order, blocks):
        route = []
        for i in range(count):
            chip = i >> 1
            target = chip - chip % group + (chip % group ^ step)
            route.append((i, target << 1 | i & 1))
        result.append(lax.ppermute(block, axis, route))
    return result


def call(kernel, out_shape, args, specs, scratch=(), flops=0, name=None, outs=VMEM, aliases={}):
    return pl.pallas_call(
        kernel,
        out_shape=out_shape,
        in_specs=specs,
        out_specs=jax.tree.map(lambda _: outs, out_shape),
        scratch_shapes=list(scratch),
        compiler_params=pltpu.CompilerParams(vmem_limit_bytes=16 << 20),
        cost_estimate=pl.CostEstimate(
            flops=flops,
            transcendentals=0,
            bytes_accessed=sum(a.size * a.dtype.itemsize for a in args),
        ),
        name=name,
        input_output_aliases=aliases,
    )(*args)


def split_heads(source, wide, heads, length, store):
    wide[...] = source[...].astype(F32)
    for head in range(heads):
        store(head, wide[pl.ds(head, length, stride=heads), :])


def level_rows(sizes, scale, position_ref, pick_ref, table_ref, tw_ref):
    heads, length, levels, block, bits = sizes
    groups = table_ref.shape[0]
    lane = lax.broadcasted_iota(jnp.int32, (groups, levels), 1)
    factor = jnp.full((groups, levels), scale, F32)
    for j in range(bits):
        flag = (position_ref[0] >> j & 1).astype(F32) * scale
        factor = jnp.where(lane == levels - bits + j, flag, factor)
    group = lax.broadcasted_iota(jnp.int32, (groups, length), 0)
    one_hot = (group == pick_ref[...]).astype(F32)
    for head in range(heads):
        table = table_ref[:, head, :] * factor
        tw_ref[head] = lax.dot_general(one_hot, table, TN, precision=exact_mode, preferred_element_type=F32)


def gain_rows(sizes, g_ref, gain_ref, gg_ref, wide):
    heads, length = sizes

    def store(head, value):
        gg_ref[head] = value * gain_ref[head:head + 1, :]
    split_heads(g_ref, wide, heads, length, store)


def local_forward(sizes, q_ref, k_ref, v_ref, tw_ref, inner_ref, p_ref, w_ref, qd_ref, kd_ref, vd_ref, wide):
    heads, length, levels, block, bits = sizes
    base = block.bit_length() - 1
    for source, target in ((k_ref, kd_ref), (v_ref, vd_ref), (q_ref, qd_ref)):
        def store(head, value, target=target):
            target[head] = value.astype(BF16)
        split_heads(source, wide, heads, length, store)
    row = lax.broadcasted_iota(jnp.int32, (block, block), 0)
    column = lax.broadcasted_iota(jnp.int32, (block, block), 1)
    differs = row ^ column
    below = column <= row
    for head in range(heads):
        for i in range(length // block):
            rows = slice(i * block, (i + 1) * block)
            reach = slice(0, (i + 1) * block)
            def weight(level):
                return tw_ref[head, rows, level:level + 1]
            diagonal = jnp.broadcast_to(weight(0), (block, block))
            for level in range(1, base + 1):
                diagonal = jnp.where(differs >= 1 << (level - 1), weight(level), diagonal)
            diagonal = jnp.where(below, diagonal, 0.0)
            w_ref[head * (length // block) + i] = diagonal
            scores = dot(qd_ref[head, rows, :], kd_ref[head, reach, :], NT)
            parts = []
            for j in range(i):
                parts.append(scores[:, j * block:(j + 1) * block] * weight(base + (i ^ j).bit_length()))
            parts.append(scores[:, rows] * diagonal)
            for j, part in enumerate(parts):
                p_ref[head, rows, j * block:(j + 1) * block] = part.astype(BF16)
            inner_ref[head, rows, :] = dot(p_ref[head, rows, reach], vd_ref[head, reach, :], NN)


def cross_heads(sizes, heads_at, held_at, inner_ref, qd_ref, gg_ref, tw_ref, attn_ref, sums_ref, add=None):
    _, length, levels, block, bits = sizes
    for i in range(length // block):
        rows = slice(i * block, (i + 1) * block)
        squares = 0.0
        products = 0.0
        for h, head in enumerate(heads_at):
            total = inner_ref[head, rows, :]
            query = qd_ref[head, rows, :]
            for j in range(bits):
                at = levels - bits + j
                total = total + tw_ref[head, rows, at:at + 1] * dot(query, held_at(j, h), NN)
            attn_ref[h, rows, :] = total
            squares = squares + total * total
            products = products + total * gg_ref[head, rows, :]
        both = (squares, products)
        for n in range(2):
            row = jnp.sum(both[n].T, axis=0, keepdims=True)
            if add is not None:
                row = row + add[n:n + 1, rows]
            sums_ref[n:n + 1, rows] = row


def cross_mine(sizes, *refs):
    heads, length, levels, block, bits = sizes
    position_ref, inner_ref, qd_ref, gg_ref, tw_ref, near_ref = refs[:6]
    mine = refs[6:6 + bits - 1]
    attn_ref, sums_ref, held_ref = refs[-3:]
    half = heads // 2
    start = (position_ref[0] & 1) * half
    for h in range(half):
        held_ref[0, h] = near_ref[start + h].astype(BF16)
        for j in range(1, bits):
            held_ref[j, h] = mine[j - 1][h].astype(BF16)
    cross_heads(sizes, [start + h for h in range(half)], lambda j, h: held_ref[j, h],
                inner_ref, qd_ref, gg_ref, tw_ref, attn_ref, sums_ref)


def cross_other(sizes, *refs):
    heads, length, levels, block, bits = sizes
    position_ref, inner_ref, qd_ref, gg_ref, tw_ref, near_ref, add_ref = refs[:7]
    other = refs[7:7 + bits - 1]
    attn_ref, sums_ref, held_ref = refs[-3:]
    half = heads // 2
    start = (1 - (position_ref[0] & 1)) * half
    for h in range(half):
        held_ref[0, h] = near_ref[start + h].astype(BF16)
        for j in range(1, bits):
            held_ref[j, h] = other[j - 1][h].astype(BF16)
    cross_heads(sizes, [start + h for h in range(half)], lambda j, h: held_ref[j, h],
                inner_ref, qd_ref, gg_ref, tw_ref, attn_ref, sums_ref, add_ref)


def sibling(source, target, place):
    return ((source >> place) == (target >> place ^ 1)).astype(F32)


def combine_kernel(group, position_ref, *refs):
    far = group.bit_length() - 1
    received, targets = refs[:group - 1], refs[group - 1:]
    chip = (position_ref[0] >> 1) & (group - 1)
    for place in range(far):
        total = 0.0
        for step, block in zip(swaps(group), received):
            source = chip ^ step
            total = total + sibling(source, chip, place) * block[...]
        targets[place][...] = total


def message_kernel(group, position_ref, above_ref, keep_ref, came_ref, *targets):
    far = group.bit_length() - 1
    chip = (position_ref[0] >> 1) & (group - 1)
    for step, message in zip(back_swaps(group), targets):
        target = chip ^ step
        total = above_ref[...]
        for place in range(far):
            total = total + sibling(chip, target, place) * (keep_ref[place] + came_ref[place])
        message[...] = total


def spread(row, width):
    return jnp.broadcast_to(row, (width, row.shape[1])).T


def token_scales(features, sums):
    total = sums[0][...]
    for part in sums[1:]:
        total = total + part[...]
    inverse = lax.rsqrt(total[0:1] / features + epsilon)
    return inverse, inverse * inverse * inverse * (total[1:2] / features)


def grad_heads(sizes, heads_at, left_at, right_at, attn_ref, gg_ref, qd_ref, tw_ref, put_grad, scaled_ref, put_state, lowest=0):
    _, length, levels, block, bits = sizes
    width = attn_ref.shape[-1]
    for h, head in enumerate(heads_at):
        for i in range(length // block):
            rows = slice(i * block, (i + 1) * block)
            grad = (left_at(rows) * gg_ref[head, rows, :] - attn_ref[h, rows, :] * right_at(rows)).astype(BF16)
            put_grad(h, rows, grad)
            wide = grad.astype(F32)
            for j in range(lowest, bits):
                at = levels - bits + j
                scaled_ref[rows, (j - lowest) * width:(j - lowest + 1) * width] = (tw_ref[head, rows, at:at + 1] * wide).astype(BF16)
        product = dot(qd_ref[head], scaled_ref[:, :(bits - lowest) * width], TN)
        for j in range(lowest, bits):
            put_state(j, h, product[:, (j - lowest) * width:(j - lowest + 1) * width])


def grad_other(sizes, features, *refs):
    heads, length, levels, block, bits = sizes
    position_ref, attn_ref, gg_ref, qd_ref, tw_ref = refs[:5]
    sums = refs[5:-6]
    ag_ref, inverse_ref, left_ref, right_ref, send_ref, scaled_ref = refs[-6:]
    half = heads // 2
    start = (1 - (position_ref[0] & 1)) * half
    width = attn_ref.shape[-1]
    inverse, beta = token_scales(features, sums)
    inverse_ref[...] = inverse
    for i in range(length // block):
        rows = slice(i * block, (i + 1) * block)
        left_ref[rows, :] = spread(inverse[:, rows], width)
        right_ref[rows, :] = spread(beta[:, rows], width)

    def put_grad(h, rows, grad):
        ag_ref[h, rows, :] = grad

    def put_state(j, h, value):
        send_ref[j - 1, h] = value
    grad_heads(sizes, [start + h for h in range(half)], lambda rows: left_ref[rows, :], lambda rows: right_ref[rows, :],
               attn_ref, gg_ref, qd_ref, tw_ref, put_grad, scaled_ref, put_state, 1)


def grad_mine(sizes, position_ref, attn_ref, far_ref, gg_ref, qd_ref, tw_ref, other_ref, left_ref, right_ref,
              held_mine_ref, held_other_ref, ag_ref, first_ref, first_far_ref, keep_ref, attn_full_ref, held_ref, scaled_ref):
    heads, length, levels, block, bits = sizes
    half = heads // 2
    core = position_ref[0] & 1
    start = core * half
    away = (1 - core) * half

    def put_grad(h, rows, grad):
        ag_ref[start + h, rows, :] = grad

    def put_state(j, h, value):
        if j == 0:
            first_ref[h] = value
        else:
            keep_ref[j - 1, h] = value
    grad_heads(sizes, [start + h for h in range(half)], lambda rows: left_ref[rows, :], lambda rows: right_ref[rows, :],
               attn_ref, gg_ref, qd_ref, tw_ref, put_grad, scaled_ref, put_state)
    for h in range(half):
        ag_ref[away + h] = other_ref[h]
        at = levels - bits
        width = other_ref.shape[-1]
        scaled_ref[:, :width] = (tw_ref[away + h, :, at:at + 1] * other_ref[h].astype(F32)).astype(BF16)
        first_far_ref[h] = dot(qd_ref[away + h], scaled_ref[:, :width], TN)
        attn_full_ref[start + h] = attn_ref[h]
        attn_full_ref[away + h] = far_ref[h]
        for j in range(bits):
            held_ref[j, start + h] = held_mine_ref[j, h]
            held_ref[j, away + h] = held_other_ref[j, h]


def local_backward(sizes, ag_ref, qd_ref, kd_ref, vd_ref, p_ref, w_ref, tw_ref, held_ref, attn_ref,
                   inverse_ref, gain_ref, normed_ref, dq_ref, dk_ref, dv_ref, weighted_ref):
    heads, length, levels, block, bits = sizes
    base = block.bit_length() - 1
    width = ag_ref.shape[-1]
    blocks = length // block
    for i in range(blocks):
        rows = slice(i * block, (i + 1) * block)
        reach = slice(0, (i + 1) * block)
        left = spread(inverse_ref[:, rows], width)
        for head in range(heads):
            put = pl.ds(i * block * heads + head, block, stride=heads)
            normed_ref[put, :] = attn_ref[head, rows, :] * left * gain_ref[head:head + 1, :]
            def weight(level):
                return tw_ref[head, rows, level:level + 1]
            grad = ag_ref[head, rows, :]
            scores = dot(grad, vd_ref[head, reach, :], NT)
            for j in range(i + 1):
                part = scores[:, j * block:(j + 1) * block]
                if j == i:
                    part = part * w_ref[head * blocks + i]
                else:
                    part = part * weight(base + (i ^ j).bit_length())
                weighted_ref[head, rows, j * block:(j + 1) * block] = part.astype(BF16)
            total = dot(weighted_ref[head, rows, reach], kd_ref[head, reach, :], NN)
            for j in range(bits):
                total = total + weight(levels - bits + j) * dot(grad, held_ref[j, head], NT)
            dq_ref[put, :] = total
    for head in range(heads):
        for j in range(blocks):
            cols = slice(j * block, (j + 1) * block)
            rest = slice(j * block, length)
            dk_ref[head, cols, :] = dot(weighted_ref[head, rest, cols], qd_ref[head, rest, :], TN)
            dv_ref[head, cols, :] = dot(p_ref[head, rest, cols], ag_ref[head, rest, :], TN)


def final_heads(sizes, start, position_ref, near_ref, total_ref, kd_ref, vd_ref, dk_ref, dv_ref,
                key_ref, value_ref, key_hbm, value_hbm, sems):
    heads, length, block = sizes
    half = heads // 2
    keep = (1 - (position_ref[0] & 1)).astype(F32)
    copies = []
    for h in range(half):
        head = start + h
        back = (total_ref[h] + keep * near_ref[h]).astype(BF16)
        key_ref[h] = dk_ref[head] + dot(vd_ref[head], back, NT)
        copies.append(pltpu.make_async_copy(key_ref.at[h], key_hbm.at[:, head, :], sems.at[0, h]))
        copies[-1].start()
        value_ref[h] = dv_ref[head] + dot(kd_ref[head], back, NN)
        copies.append(pltpu.make_async_copy(value_ref.at[h], value_hbm.at[:, head, :], sems.at[1, h]))
        copies[-1].start()
    for copy in copies:
        copy.wait()


def final_mine(sizes, position_ref, *refs):
    final_heads(sizes, (position_ref[0] & 1) * (sizes[0] // 2), position_ref, *refs[:6], *refs[8:10], *refs[6:8], refs[10])


def final_other(sizes, position_ref, *refs):
    start = (1 - (position_ref[0] & 1)) * (sizes[0] // 2)
    final_heads(sizes, start, position_ref, *refs[:6], *refs[10:12], *refs[8:10], refs[12])


def shards(query_rows, key_rows, value_rows, level_pick, level_table, norm_gain, out_grad):
    length, heads, width = query_rows.shape
    groups, _, levels = level_table.shape
    local_bits = length.bit_length() - 1
    bits = lax.axis_size("seq").bit_length() - 1
    block = min(128, length)
    half = heads // 2
    scale = width ** (-0.5)
    position = lax.axis_index("seq").astype(jnp.int32)
    place_arg = position.reshape(1)
    shape = jax.ShapeDtypeStruct

    own = jnp.einsum("shd,she->hde", key_rows, value_rows, preferred_element_type=F32)
    near = swapped(own, "seq", 0)
    sizes = (heads, length, levels, block, bits)
    rows = length * heads
    flat = lambda a: a.reshape(rows, width)
    local_flops = heads * length * length * width
    weights = call(
        functools.partial(level_rows, sizes, scale),
        shape((heads, length, levels), F32),
        (place_arg, level_pick.reshape(1, length), level_table),
        [SMEM, VMEM, VMEM],
        name="level_rows",
    )
    pair = own + near

    block_sum = lax.dynamic_slice(
        pair, ((position & 1) * half, 0, 0), (half, width, width), allow_negative_indices=False
    )
    far = min(bits - 1, 2)
    group = 1 << far
    received = turned([block_sum] * (group - 1), "seq", group, swaps(group))

    inner, probs, diag, qd, kd, vd = call(
        functools.partial(local_forward, sizes),
        (
            shape((heads, length, width), F32),
            shape((heads, length, length), BF16),
            shape((heads * (length // block), block, block), F32),
            shape((heads, length, width), BF16),
            shape((heads, length, width), BF16),
            shape((heads, length, width), BF16),
        ),
        (flat(query_rows), flat(key_rows), flat(value_rows), weights),
        [VMEM] * 4,
        [pltpu.VMEM((rows, width), F32)],
        flops=4 * local_flops,
        name="local_forward",
    )
    gg = call(
        functools.partial(gain_rows, (heads, length)),
        shape((heads, length, width), F32),
        (flat(out_grad), norm_gain),
        [VMEM] * 2,
        [pltpu.VMEM((rows, width), F32)],
        name="gain_rows",
    )
    inner, gg, received = lax.optimization_barrier((inner, gg, received))
    state = shape((half, width, width), F32)
    mine = call(
        functools.partial(combine_kernel, group),
        (state,) * far,
        (place_arg, *received),
        [SMEM] + [VMEM] * (group - 1),
        name="far_states",
    )
    mine = list(mine)
    block_sum = functools.reduce(jnp.add, received, block_sum)
    for place in range(far + 1, bits):
        mine.append(swapped(block_sum, "seq", place))
        block_sum = block_sum + mine[-1]
    others = [swapped(partner, "seq", 0) for partner in mine]
    cross_flops = bits * heads * length * width * width
    cross_shapes = (
        shape((half, length, width), F32),
        shape((2, length), F32),
        shape((bits, half, width, width), BF16),
    )
    attn_mine, sums, held_mine = call(
        functools.partial(cross_mine, sizes),
        cross_shapes,
        (place_arg, inner, qd, gg, weights, near, *mine),
        [SMEM] + [VMEM] * (5 + len(mine)),
        flops=cross_flops,
        name="cross_mine",
    )
    attn_other, sums, held_other = call(
        functools.partial(cross_other, sizes),
        cross_shapes,
        (place_arg, inner, qd, gg, weights, near, sums, *others),
        [SMEM] + [VMEM] * (6 + len(others)),
        flops=cross_flops,
        name="cross_other",
    )
    features = heads * width * lax.axis_size("heads")
    parts = summands(sums, "heads")
    grad_far, inverse, left, right, send = call(
        functools.partial(grad_other, sizes, features),
        (
            shape((half, length, width), BF16),
            shape((1, length), F32),
            shape((length, width), F32),
            shape((length, width), F32),
            shape((bits - 1, half, width, width), F32),
        ),
        (place_arg, attn_other, gg, qd, weights, *parts),
        [SMEM] + [VMEM] * (4 + len(parts)),
        [pltpu.VMEM((length, bits * width), BF16)],
        flops=cross_flops,
        name="state_grads_other",
    )
    attn_grad, first_mine, first_other, keep, attn, held = call(
        functools.partial(grad_mine, sizes),
        (
            shape((heads, length, width), BF16),
            shape((half, width, width), F32),
            shape((half, width, width), F32),
            shape((bits - 1, half, width, width), F32),
            shape((heads, length, width), F32),
            shape((bits, heads, width, width), BF16),
        ),
        (place_arg, attn_mine, attn_other, gg, qd, weights, grad_far, left, right, held_mine, held_other),
        [SMEM] + [VMEM] * 10,
        [pltpu.VMEM((length, bits * width), BF16)],
        flops=cross_flops,
        name="state_grads_mine",
    )
    came = swapped(send, "seq", 0)
    above = jnp.zeros((half, width, width), F32)
    for place in reversed(range(far + 1, bits)):
        above = above + swapped(above + keep[place - 1] + came[place - 1], "seq", place)
    messages = call(
        functools.partial(message_kernel, group),
        (state,) * (group - 1),
        (place_arg, above, keep, came),
        [SMEM] + [VMEM] * 3,
        name="far_messages",
    )
    landed = turned(messages, "seq", group, back_swaps(group))
    near_other = swapped(first_mine, "seq", 0)
    near_mine = swapped(first_other, "seq", 0)

    normed, query_grad, key_part, value_part = call(
        functools.partial(local_backward, sizes),
        (
            shape((rows, width), F32),
            shape((rows, width), F32),
            shape((heads, length, width), F32),
            shape((heads, length, width), F32),
        ),
        (attn_grad, qd, kd, vd, probs, diag, weights, held, attn, inverse, norm_gain),
        [VMEM] * 11,
        [pltpu.VMEM((heads, length, length), BF16)],
        flops=8 * local_flops,
        name="local_backward",
    )
    landed, key_part = lax.optimization_barrier((landed, key_part))
    total = functools.reduce(jnp.add, landed, above)
    other = swapped(total, "seq", 0)

    final_sizes = (heads, length, block)
    final_flops = 2 * heads * length * width * width
    whole = (shape((length, heads, width), F32), shape((length, heads, width), F32))
    scratch = [
        pltpu.VMEM((half, length, width), F32),
        pltpu.VMEM((half, length, width), F32),
        pltpu.SemaphoreType.DMA((2, half)),
    ]
    started = call(
        functools.partial(final_mine, final_sizes),
        whole,
        (place_arg, near_mine, total, kd, vd, key_part, value_part),
        [SMEM] + [VMEM] * 6,
        scratch,
        flops=final_flops,
        name="key_value_mine",
        outs=HBM,
    )
    key_grad, value_grad = call(
        functools.partial(final_other, final_sizes),
        whole,
        (place_arg, near_other, other, kd, vd, key_part, value_part, *started),
        [SMEM] + [VMEM] * 6 + [HBM] * 2,
        scratch,
        flops=final_flops,
        name="key_value_other",
        outs=HBM,
        aliases={7: 0, 8: 1},
    )
    return tuple(a.reshape(length, heads, width) for a in (normed, query_grad, key_grad, value_grad))


def solution(mesh):
    in_specs = (
        P("seq", "heads", None),
        P("seq", "heads", None),
        P("seq", "heads", None),
        P("seq"),
        P(None, "heads", None),
        P("heads", None),
        P("seq", "heads", None),
    )
    out_specs = (
        P("seq", "heads", None),
        P("seq", "heads", None),
        P("seq", "heads", None),
        P("seq", "heads", None),
    )
    return jax.shard_map(shards, mesh=mesh, in_specs=in_specs, out_specs=out_specs, check_vma=False)
```
